256 devices in a mesh: tm: 4 (over z_lo), space: 64 (over y, x, z_hi, core).
Axes of the slice: x: 4, y: 4, z: 8 (z_hi: 2, z_lo: 4; z = z_hi * 4 + z_lo), core: 2. Of those that a mesh axis runs over, the one named last changes fastest.
Arguments:
- initial: float32 [256, 256, 512], P('space'), may hold values from -6 to 6
- iterate: float32 [4, 256, 256, 512], P('tm', 'space'), may hold values from -6 to 6
- diffusivity: float32 [256, 256, 512], P('space'), may hold values from 0.25 to 1
Outputs:
- corrected: float32 [4, 256, 256, 512], P('tm', 'space')
The draws below stay inside these ranges and needn't reach their ends.
All inputs are finite; a program needn't handle non-finite values.
Results may differ from the reference program's by a relative error of at most 0.0001.
Values sent between devices are 32-bit elements; how exact they have to be, the bound alone decides.
A program may use at most 128 MiB of HBM per device.

```python
import math
import jax
import jax.numpy as jnp

NY = 256
NX = 512
STEPS = 4
NZ = 256
INTERVALS = 4
N_TM = 4


def block_scale(own_key, shape, pieces, smallest, high):
    loudness, own = 1.0, jax.random.fold_in(own_key, 6)
    for position, shards_of in pieces:
        draws = jnp.exp(jax.random.uniform(jax.random.fold_in(own, position), (shards_of,), jnp.float32, smallest / len(pieces), high / len(pieces)))
        loudness = loudness * jnp.repeat(draws, shape[position] // shards_of).reshape([-1 if axis == position else 1 for axis in range(len(shape))])
    return loudness


def gaussian(own_key, shape, scale, reach, shards=(), dtype=jnp.bfloat16):
    factor_of = block_scale(own_key, shape, shards, -0.22, 0.18) if shards else 1.0
    drawn = jax.random.normal(own_key, shape, jnp.float32) * scale * factor_of
    return jnp.minimum(jnp.maximum(drawn, -reach), reach).astype(dtype)


def setup_inputs(seed: int = 0) -> dict:
    splits = jax.random.split(jax.random.key(seed), 4)
    return {
        "initial": gaussian(splits[0], (NZ, NY, NX), 1.0, 6.0, ((0, 64),), jnp.float32),
        "iterate": gaussian(splits[1], (INTERVALS, NZ, NY, NX), 1.0, 6.0, ((0, 4), (1, 64)), jnp.float32),
        "diffusivity": jnp.clip(jnp.exp(math.log(1.0) - 1.3862944 * jax.random.uniform(splits[2], (NZ, NY, NX), jnp.float32) ** block_scale(splits[2], (NZ, NY, NX), ((0, 64),), -0.2, 0.2)), 0.25, 1.0),
    }


courant = 0.15


def advance(values, diffusivity):
    center = values[1:-1]
    coeff = diffusivity[1:-1]
    flux = (coeff + diffusivity[2:]) * (values[2:] - center) + (coeff + diffusivity[:-2]) * (values[:-2] - center)
    side_values = jnp.pad(center, ((0, 0), (1, 1), (0, 0)))
    side_coeff = jnp.pad(coeff, ((0, 0), (1, 1), (0, 0)))
    flux = flux + (coeff + side_coeff[:, 2:]) * (side_values[:, 2:] - center) + (coeff + side_coeff[:, :-2]) * (side_values[:, :-2] - center)
    cross_values = jnp.pad(center, ((0, 0), (0, 0), (1, 1)))
    cross_coeff = jnp.pad(coeff, ((0, 0), (0, 0), (1, 1)))
    flux = flux + (coeff + cross_coeff[:, :, 2:]) * (cross_values[:, :, 2:] - center) + (coeff + cross_coeff[:, :, :-2]) * (cross_values[:, :, :-2] - center)
    return center + (0.5 * courant) * flux


def zpad(values):
    return jnp.pad(values, ((1, 1), (0, 0), (0, 0)))


def restrict(values):
    depth_z, depth_y, depth_x = values.shape
    return values.reshape(depth_z // 2, 2, depth_y // 2, 2, depth_x // 2, 2).mean(axis=(1, 3, 5))


def prolong(values):
    depth_z, depth_y, depth_x = values.shape
    spread = jnp.broadcast_to(values[:, None, :, None, :, None], (depth_z, 2, depth_y, 2, depth_x, 2))
    return spread.reshape(2 * depth_z, 2 * depth_y, 2 * depth_x)


def reference(initial, iterate, diffusivity):
    padded_diff = zpad(diffusivity)
    padded_coarse = zpad(restrict(diffusivity))
    error = jnp.zeros((NZ // 2, NY // 2, NX // 2), jnp.float32)
    outputs = []
    begin_state = initial
    for interval in range(N_TM):
        state = begin_state
        for number in range(STEPS):
            state = advance(zpad(state), padded_diff)
        residual = state - iterate[interval]
        error = advance(zpad(error), padded_coarse) + restrict(residual)
        outputs.append(iterate[interval] + prolong(error))
        begin_state = iterate[interval]
    return jnp.stack(outputs)
```

```python
import jax
import jax.numpy as jnp
from jax import lax
from jax.experimental import pallas as pl
from jax.experimental.pallas import tpu as pltpu
from jax.sharding import PartitionSpec as P

STEPS = 4
courant = 0.15
K = 0.5 * courant
F32 = jnp.float32
MESH = pl.DeviceIdType.MESH

Y, X = 256, 512
LT = X // 128
R = 32
RC = 16
CH = 12


def lanes(shape):
    return lax.broadcasted_iota(jnp.int32, shape, 1)


def subs(shape):
    return lax.broadcasted_iota(jnp.int32, shape, 0)


def at_right(v, by):
    n = v.shape[1]
    return jnp.where(lanes(v.shape) >= n - by, 0.0, pltpu.roll(v, n - by, axis=1))


def at_left(v, by):
    return jnp.where(lanes(v.shape) < by, 0.0, pltpu.roll(v, by, axis=1))


def from_below(v):
    return jnp.where(subs(v.shape) == 7, 0.0, pltpu.roll(v, 7, axis=0))


def from_above(v):
    return jnp.where(subs(v.shape) == 0, 0.0, pltpu.roll(v, 1, axis=0))


def even(shape):
    return (lanes(shape) & 1) == 0


def swap_pairs(v):
    n = v.shape[1]
    return jnp.where(even(v.shape), pltpu.roll(v, n - 1, axis=1), pltpu.roll(v, 1, axis=1))


def pack(a, b):
    n = a.shape[1]
    return jnp.where(even(a.shape), a + pltpu.roll(a, n - 1, axis=1), b + pltpu.roll(b, 1, axis=1))


def coarse_advance(c, c_up, c_dn, c_io, v, v_up, v_dn, v_io):
    flux = (c + at_right(c, 2)) * (at_right(v, 2) - v) + (c + at_left(c, 2)) * (at_left(v, 2) - v)
    flux = flux + (c + c_up) * (v_up - v) + (c + c_dn) * (v_dn - v)
    flux = flux + (c + swap_pairs(c)) * (swap_pairs(v) - v)
    flux = flux + (c + c_io) * (v_io - v)
    return v + K * flux


def main_kernel(
    ini,
    itr,
    dif,
    out,
    craw,
    uraw,
    cbuf,
    dg,
    kxp,
    kxm,
    ky,
    kz,
    w,
    inn,
    cc,
    ccp,
    icoarse,
    ipart,
    own,
    ext,
    ccb,
    cco,
    go,
    gx,
    eb,
    hlo,
    hhi,
    hp,
    hn,
    eout,
    ld_sem,
    icp,
    chs,
    chr_,
    ins,
    inr,
    pps,
    ppr,
    cbs,
    cbr,
    cor,
    gos,
    gor,
    gxs,
    gxr,
    hs,
    hr,
    eos,
    eor,
):
    t = lax.axis_index("tm")
    s = lax.axis_index("space")
    core = s % 2
    zhi = (s // 2) % 2
    col = s // 4
    z = zhi * 4 + t
    ncol = lax.axis_size("space") // 4
    partner = s + 1 - 2 * core
    cross_ok = jnp.logical_and(
        jnp.logical_or(core == 1, s > 0), jnp.logical_or(core == 0, s < 4 * ncol - 1)
    )
    cross = jnp.where(cross_ok, s - 1 + 2 * core, s)
    qcol = cross // 4
    qzhi = (cross // 2) % 2
    qcore = cross % 2

    def plane(p):
        return (3 - p) + core * (2 * p - 3)

    def dev(tt, ss):
        return {"tm": tt, "space": ss}

    barrier = pltpu.get_barrier_semaphore()

    @pl.loop(0, 16)
    def _(i):
        ti, si = i % 4, col * 4 + i // 4

        @pl.when(jnp.logical_not(jnp.logical_and(ti == t, si == s)))
        def _():
            pl.semaphore_signal(barrier, inc=1, device_id=dev(ti, si), device_id_type=MESH)

    lat_ok = jnp.logical_or(
        jnp.logical_and(core == 0, col > 0), jnp.logical_and(core == 1, col < ncol - 1)
    )
    lat_col = jnp.where(core == 0, col - 1, col + 1)

    @pl.when(lat_ok)
    def _():
        @pl.loop(0, 8)
        def _(i):
            si = lat_col * 4 + (i // 4) * 2 + 1 - core
            pl.semaphore_signal(barrier, inc=1, device_id=dev(i % 4, si), device_id_type=MESH)

    def own_c(p, q):
        return pltpu.make_async_copy(
            dif.at[plane(p), :, pl.ds(128 * q, 128)], craw.at[p, q], ld_sem.at[0]
        )

    def own_u(src, p, q):
        return pltpu.make_async_copy(
            src.at[plane(p), :, pl.ds(128 * q, 128)], uraw.at[p, q], ld_sem.at[1]
        )

    for p in range(4):
        for q in range(LT):
            own_c(p, q).start()

    @pl.when(t == 3)
    def _():
        for p in range(4):
            for q in range(LT):
                own_u(ini, p, q).start()

    @pl.when(t != 3)
    def _():
        for p in range(4):
            for q in range(LT):
                own_u(itr.at[0], p, q).start()

    pl.semaphore_wait(barrier, jnp.where(lat_ok, 23, 15))

    def inner_c(q):
        return pltpu.make_async_remote_copy(
            src_ref=dif.at[plane(0), :, pl.ds(128 * q, 128)],
            dst_ref=craw.at[7, q],
            send_sem=icp.at[0, q],
            recv_sem=icp.at[1, q],
            device_id=dev(t, partner),
            device_id_type=MESH,
        )

    for q in range(LT):
        inner_c(q).start()

    def first(ch, i):
        j, q = i // LT, i % LT
        return pltpu.make_async_remote_copy(
            src_ref=dif.at[plane(3 - j), pl.ds(128 * ch, 128), pl.ds(pl.multiple_of(128 * q, 128), 128)],
            dst_ref=craw.at[4 + j, q, pl.ds(128 * ch, 128), :],
            send_sem=chs.at[2 + ch, i],
            recv_sem=chr_.at[ch, i],
            device_id=dev(3 - 3 * ch, cross),
            device_id_type=MESH,
        )

    def relay(ch, i):
        j, q = i // LT, i % LT
        ref = craw.at[4 + j, q, pl.ds(128 * ch, 128), :]
        return pltpu.make_async_remote_copy(
            src_ref=ref,
            dst_ref=ref,
            send_sem=chs.at[ch, i],
            recv_sem=chr_.at[ch, i],
            device_id=dev(jnp.clip(t - 1 + 2 * ch, 0, 3), s),
            device_id_type=MESH,
        )

    starts = (t == 0, t == 3)
    sends_on = (t > 0, t < 3)

    @pl.when(cross_ok)
    def _():
        for ch in range(2):

            @pl.when(starts[ch])
            def _():
                @pl.loop(0, CH)
                def _(i):
                    first(ch, i).start()

    def to_rows(raw, p, dst, d):
        for q in range(LT):

            @pl.loop(0, R)
            def _(r):
                dst[d, r + 1, :, 128 * q : 128 * q + 128] = raw[p, q, pl.ds(r, 8, stride=R), :]

        edge_rows(dst, d)

    def edge_rows(dst, d):
        dst[d, 0] = from_above(dst[d, R])
        dst[d, R + 1] = from_below(dst[d, 1])

    held_c = craw.at[pl.ds(0, 4)]
    pltpu.make_async_copy(held_c, held_c, ld_sem.at[0]).wait()
    pltpu.make_async_copy(uraw, uraw, ld_sem.at[1]).wait()
    for p in range(4):
        to_rows(uraw, p, w.at[0], p)

    def inner_state(k):
        return pltpu.make_async_remote_copy(
            src_ref=w.at[k % 2, 0, pl.ds(1, R)],
            dst_ref=inn.at[k],
            send_sem=ins.at[k],
            recv_sem=inr.at[k],
            device_id=dev(t, partner),
            device_id_type=MESH,
        )

    inner_state(0).start()
    for p in range(4):
        to_rows(craw, p, cbuf, p)

    @pl.loop(0, RC)
    def _(r):
        def block(src, p):
            a = 2 * r + 1
            return (src[p, a] + src[p, a + 1]) + (src[p + 1, a] + src[p + 1, a + 1])

        cc[r] = 0.125 * pack(block(cbuf, 0), block(cbuf, 2))
        icoarse[r] = 0.125 * pack(block(w.at[0], 0), block(w.at[0], 2))

    def to_partner(i):
        src, dst = ((cc, ccp), (icoarse, ipart))[i]
        return pltpu.make_async_remote_copy(
            src_ref=src,
            dst_ref=dst,
            send_sem=pps.at[i],
            recv_sem=ppr.at[i],
            device_id=dev(t, partner),
            device_id_type=MESH,
        )

    to_partner(0).start()
    to_partner(1).start()

    off = (jnp.where(t == 0, 5, jnp.where(t == 1, 1, 0)), jnp.where(t == 3, 5, jnp.where(t == 2, 1, 0)))

    @pl.when(cross_ok)
    def _():
        @pl.loop(0, CH + 5)
        def _(n):
            for ch in range(2):
                i = n - off[ch]

                @pl.when(jnp.logical_and(i >= 0, i < CH))
                def _():
                    relay(ch, i).wait_recv()

                    @pl.when(sends_on[ch])
                    def _():
                        relay(ch, i).start()

    for q in range(LT):
        inner_c(q).wait_recv()
    to_rows(craw, 7, cbuf, 7)

    @pl.when(cross_ok)
    def _():
        for p in range(4, 7):
            to_rows(craw, p, cbuf, p)

    @pl.when(jnp.logical_not(cross_ok))
    def _():
        for p in range(4, 7):

            @pl.loop(0, R + 2)
            def _(r):
                cbuf[p, r] = jnp.zeros((8, X), F32)

    def cross_send(is_self, src, dst, ssem, rsem, to):
        @pl.when(is_self)
        def _():
            pltpu.make_async_copy(src, dst, rsem).start()

        @pl.when(jnp.logical_not(is_self))
        def _():
            pltpu.make_async_remote_copy(
                src_ref=src,
                dst_ref=dst,
                send_sem=ssem,
                recv_sem=rsem,
                device_id=to,
                device_id_type=MESH,
            ).start()

    def cross_sent(is_self, src, dst, ssem, rsem, to):
        @pl.when(jnp.logical_not(is_self))
        def _():
            pltpu.make_async_remote_copy(
                src_ref=src,
                dst_ref=dst,
                send_sem=ssem,
                recv_sem=rsem,
                device_id=to,
                device_id_type=MESH,
            ).wait_send()

    def cc_own(h, m):
        e = t + 4 * h
        sp = col * 4 + h * 2 + zhi
        row = (2 * e - 1 + m + RC) % RC
        return sp == s, cc.at[row], ccb.at[core, m], cbs.at[h, m], cbr.at[0], dev(t, sp)

    def cc_out(h):
        e = t + 4 * h
        sp = qcol * 4 + h * 2 + qzhi
        return sp == s, cc.at[pl.ds(2 * e, 2)], cco.at[qcore], cbs.at[h, 4], cor.at[qcore], dev(t, sp)

    for h in range(2):
        for m in range(4):
            cross_send(*cc_own(h, m))

        @pl.when(cross_ok)
        def _():
            cross_send(*cc_out(h))

    vflag = jnp.where(cross_ok, 1.0, 0.0).astype(F32)

    @pl.loop(0, R)
    def _(r):
        a = r + 1
        ln = lanes((8, X))
        czm = cbuf[7, a]
        c = cbuf[0, a]
        kzm = K * (czm + c)
        for p in range(7):
            right = K * (c + at_right(c, 1))
            left = K * (c + at_left(c, 1))
            up = K * (c + cbuf[p, a + 1])
            dn = K * (c + cbuf[p, a - 1])
            total = (right + left) + (up + dn) + kzm
            kxp[p, r] = jnp.where(ln == X - 1, 0.0, right)
            kxm[p, r] = jnp.where(ln == 0, 0.0, left)
            ky[p, r] = dn
            kz[p, r] = kzm * vflag if p == 4 else kzm
            if p < 6:
                cn = cbuf[p + 1, a]
                kzm = K * (c + cn)
                total = total + kzm
                c = cn
            dg[p, r] = 1.0 - total

    for p in range(7):
        ky[p, R] = K * (cbuf[p, R] + cbuf[p, R + 1])

    def cell(k, p, r, top):
        a = r + 1
        src = w.at[k % 2]
        v = src[p, a]
        new = dg[p, r] * v
        new = new + kxp[p, r] * pltpu.roll(v, X - 1, axis=1)
        new = new + kxm[p, r] * pltpu.roll(v, 1, axis=1)
        new = new + ky[p, r + 1] * src[p, a + 1]
        new = new + ky[p, r] * src[p, a - 1]
        below = inn[k, r] if p == 0 else src[p - 1, a]
        new = new + kz[p, r] * below
        if p < top:
            new = new + kz[p + 1, r] * src[p + 1, a]
        return new

    for k in range(STEPS - 1):
        top = 3 + k
        inner_state(k).wait_recv()
        dst = w.at[(k + 1) % 2]
        if k > 0:
            inner_state(k - 1).wait_send()

        @pl.loop(0, R)
        def _(r):
            dst[0, r + 1] = cell(k, 0, r, top)

        edge_rows(dst, 0)
        inner_state(k + 1).start()

        @pl.loop(0, R)
        def _(r):
            for p in range(1, top + 1):
                dst[p, r + 1] = cell(k, p, r, top)
            dst[top + 1, r + 1] = kz[top + 1, r] * w[k % 2, top, r + 1]

        for p in range(1, top + 2):
            edge_rows(dst, p)

    to_partner(0).wait_recv()
    to_partner(1).wait_recv()
    gflag = jnp.where(t == 3, 0.0, 1.0).astype(F32)
    inner_state(STEPS - 1).wait_recv()

    @pl.loop(0, RC)
    def _(rc):
        k = STEPS - 1
        acc = []
        for planes in ((0, 1), (2, 3), (4, 5), (6,)):
            tot = None
            for p in planes:
                for b in range(2):
                    v = cell(k, p, 2 * rc + b, 6)
                    tot = v if tot is None else tot + v
            acc.append(tot)
        ev = even((8, X))
        lo = jnp.maximum(rc - 1, 0)
        hi = jnp.minimum(rc + 1, RC - 1)

        def neighbours(ref):
            up, dn = ref[hi], ref[lo]
            up = jnp.where(rc == RC - 1, from_below(ref[0]), up)
            dn = jnp.where(rc == 0, from_above(ref[RC - 1]), dn)
            return up, dn

        a = 2 * rc + 1
        outer = (cbuf[4, a] + cbuf[4, a + 1]) + (cbuf[5, a] + cbuf[5, a + 1])
        c = cc[rc]
        c_up, c_dn = neighbours(cc)
        c_io = jnp.where(ev, ccp[rc], 0.125 * pack(outer, outer))
        v = icoarse[rc]
        v_up, v_dn = neighbours(icoarse)
        v_io = jnp.where(ev, ipart[rc], 0.0)
        back = coarse_advance(c, c_up, c_dn, c_io, v, v_up, v_dn, v_io)
        own[rc] = 0.125 * pack(acc[0], acc[1]) - gflag * back
        ext[rc] = 0.125 * pack(acc[3], acc[2]) - gflag * jnp.where(ev, 0.0, K * (c + c_io) * v)

    def o_send(e):
        sp = col * 4 + (e // 4) * 2 + zhi
        te = e % 4
        return (
            jnp.logical_and(sp == s, te == t),
            own.at[pl.ds(2 * e, 2)],
            go.at[t, core],
            gos.at[e],
            gor.at[0],
            dev(te, sp),
        )

    def x_send(e):
        sp = qcol * 4 + (e // 4) * 2 + qzhi
        te = e % 4
        return (
            jnp.logical_and(sp == s, te == t),
            ext.at[pl.ds(2 * e, 2)],
            gx.at[qcore, t],
            gxs.at[e],
            gxr.at[qcore],
            dev(te, sp),
        )

    @pl.loop(0, 8)
    def _(i):
        e = (z + 4 + i) % 8
        cross_send(*o_send(e))

        @pl.when(cross_ok)
        def _():
            cross_send(*x_send(e))

    prev_ok = jnp.logical_or(core == 1, col > 0)
    next_ok = jnp.logical_or(core == 0, col < ncol - 1)
    prev_sp = jnp.where(core == 1, s - 1, jnp.maximum(col - 1, 0) * 4 + zhi * 2 + 1)
    next_sp = jnp.where(core == 0, s + 1, jnp.minimum(col + 1, ncol - 1) * 4 + zhi * 2)
    side_ok = (prev_ok, next_ok)

    pltpu.make_async_copy(ccb, ccb, cbr.at[0]).wait()
    for j in range(2):

        @pl.when(side_ok[j])
        def _():
            pltpu.make_async_copy(cco.at[j], cco.at[j], cor.at[j]).wait()

        @pl.when(jnp.logical_not(side_ok[j]))
        def _():
            cco[j] = jnp.zeros((2, 8, X), F32)
            gx[j] = jnp.zeros((4, 2, 8, X), F32)

    pltpu.make_async_copy(go, go, gor.at[0]).wait()
    for j in range(2):

        @pl.when(side_ok[j])
        def _():
            pltpu.make_async_copy(gx.at[j], gx.at[j], gxr.at[j]).wait()

    zu, zd = (z + 1) % 8, (z + 7) % 8

    def e_halo(k, kind):
        if kind == 0:
            src, dst, to = eb.at[k, 0], hhi.at[k], dev(zd % 4, col * 4 + (zd // 4) * 2 + core)
        elif kind == 1:
            src, dst, to = eb.at[k, 1], hlo.at[k], dev(zu % 4, col * 4 + (zu // 4) * 2 + core)
        elif kind == 2:
            src, dst, to = eb.at[k, :, 0], hn.at[k], dev(t, prev_sp)
        else:
            src, dst, to = eb.at[k, :, 1], hp.at[k], dev(t, next_sp)
        return pltpu.make_async_remote_copy(
            src_ref=src,
            dst_ref=dst,
            send_sem=hs.at[k, kind],
            recv_sem=hr.at[k, kind],
            device_id=to,
            device_id_type=MESH,
        )

    def e_back(k, j):
        sp = col * 4 + core * 2 + j
        return (
            jnp.logical_and(sp == s, t == k),
            eb.at[k, :, j],
            eout.at[pl.ds(2 * z, 2)],
            eos.at[k, j],
            eor.at[0],
            dev(k, sp),
        )

    for b in range(2):
        for j in range(2):
            eb[0, b, j] = go[3, j, b] + gx[j, 3, b]

    def send_level(k):
        if k < 3:
            e_halo(k, 0).start()
            e_halo(k, 1).start()

            @pl.when(prev_ok)
            def _():
                e_halo(k, 2).start()

            @pl.when(next_ok)
            def _():
                e_halo(k, 3).start()

        for j in range(2):
            cross_send(*e_back(k, j))

    send_level(0)
    for k in range(3):
        e_halo(k, 0).wait_recv()
        e_halo(k, 1).wait_recv()

        @pl.when(next_ok)
        def _():
            e_halo(k, 2).wait_recv()

        @pl.when(prev_ok)
        def _():
            e_halo(k, 3).wait_recv()

        @pl.when(jnp.logical_not(next_ok))
        def _():
            hn[k] = jnp.zeros((2, 8, X), F32)

        @pl.when(jnp.logical_not(prev_ok))
        def _():
            hp[k] = jnp.zeros((2, 8, X), F32)

        ev = even((8, X))
        for j in range(2):
            lo = hlo[k, j]
            hi = hhi[k, j]
            lo = jnp.where(z == 0, from_above(lo), lo)
            hi = jnp.where(z == 7, from_below(hi), hi)
            c_lo = jnp.where(z == 0, from_above(ccb[j, 0]), ccb[j, 0])
            c_hi = jnp.where(z == 7, from_below(ccb[j, 3]), ccb[j, 3])
            vs = (lo, eb[k, 0, j], eb[k, 1, j], hi)
            cs = (c_lo, ccb[j, 1], ccb[j, 2], c_hi)
            for b in range(2):
                far = hp[k, b] if j == 0 else hn[k, b]
                v_io = jnp.where(ev, eb[k, b, 1 - j], far)
                c_io = jnp.where(ev, ccb[1 - j, b + 1], cco[j, b])
                new = coarse_advance(
                    cs[b + 1], cs[b + 2], cs[b], c_io, vs[b + 1], vs[b + 2], vs[b], v_io
                )
                eb[k + 1, b, j] = new + (go[k, j, b] + gx[j, k, b])
        send_level(k + 1)

    pltpu.make_async_copy(eout, eout, eor.at[0]).wait()
    out[...] = eout[...]

    for q in range(LT):
        inner_c(q).wait_send()
    for k in range(STEPS - 2, STEPS):
        inner_state(k).wait_send()
    for i in range(2):
        to_partner(i).wait_send()

    @pl.when(cross_ok)
    def _():
        for ch in range(2):

            @pl.when(starts[ch])
            def _():
                @pl.loop(0, CH)
                def _(i):
                    first(ch, i).wait_send()

            @pl.when(sends_on[ch])
            def _():
                @pl.loop(0, CH)
                def _(i):
                    relay(ch, i).wait_send()

    for h in range(2):
        for m in range(4):
            cross_sent(*cc_own(h, m))

        @pl.when(cross_ok)
        def _():
            cross_sent(*cc_out(h))

    @pl.loop(0, 8)
    def _(e):
        cross_sent(*o_send(e))

        @pl.when(cross_ok)
        def _():
            cross_sent(*x_send(e))

    for k in range(3):
        e_halo(k, 0).wait_send()
        e_halo(k, 1).wait_send()

        @pl.when(prev_ok)
        def _():
            e_halo(k, 2).wait_send()

        @pl.when(next_ok)
        def _():
            e_halo(k, 3).wait_send()

    for k in range(4):
        for j in range(2):
            cross_sent(*e_back(k, j))


def final_kernel(itr, e, out, raw, res, isem, osem):
    core = lax.axis_index("space") % 2

    def plane(p):
        return (3 - p) + core * (2 * p - 3)

    def load(q):
        return pltpu.make_async_copy(itr.at[0, :, :, pl.ds(128 * q, 128)], raw.at[q], isem.at[q])

    def store(q):
        return pltpu.make_async_copy(res.at[q], out.at[0, :, :, pl.ds(128 * q, 128)], osem.at[q])

    for q in range(LT):
        load(q).start()
    for q in range(LT):
        load(q).wait()

        @pl.loop(0, RC)
        def _(r):
            rows = [[raw[q, plane(p), pl.ds(2 * r + b, 8, stride=R), :] for b in range(2)] for p in range(4)]
            a = (rows[0][0] + rows[0][1]) + (rows[1][0] + rows[1][1])
            c = (rows[2][0] + rows[2][1]) + (rows[3][0] + rows[3][1])
            d = e[r, :, 128 * q : 128 * q + 128] - 0.125 * pack(a, c)
            ev = even(d.shape)
            halves = (
                jnp.where(ev, d, pltpu.roll(d, 1, axis=1)),
                jnp.where(ev, pltpu.roll(d, 127, axis=1), d),
            )
            for p in range(4):
                for b in range(2):
                    res[q, plane(p), pl.ds(2 * r + b, 8, stride=R), :] = rows[p][b] + halves[p // 2]

        store(q).start()
    for q in range(LT):
        store(q).wait()


def local(initial, iterate, diffusivity):
    vm = lambda *shape: pltpu.VMEM(shape, F32)
    dma = lambda *shape: pltpu.SemaphoreType.DMA(shape)
    hbm = pl.BlockSpec(memory_space=pl.ANY)
    vmem = pl.BlockSpec(memory_space=pltpu.VMEM)
    err = pl.pallas_call(
        main_kernel,
        out_shape=jax.ShapeDtypeStruct((RC, 8, X), F32),
        in_specs=[hbm] * 3,
        out_specs=vmem,
        scratch_shapes=[
            vm(8, LT, Y, 128),
            vm(4, LT, Y, 128),
            vm(8, R + 2, 8, X),
            vm(7, R, 8, X),
            vm(7, R, 8, X),
            vm(7, R, 8, X),
            vm(7, R + 1, 8, X),
            vm(7, R, 8, X),
            vm(2, 7, R + 2, 8, X),
            vm(STEPS, R, 8, X),
            vm(RC, 8, X),
            vm(RC, 8, X),
            vm(RC, 8, X),
            vm(RC, 8, X),
            vm(RC, 8, X),
            vm(RC, 8, X),
            vm(2, 4, 8, X),
            vm(2, 2, 8, X),
            vm(4, 2, 2, 8, X),
            vm(2, 4, 2, 8, X),
            vm(4, 2, 2, 8, X),
            vm(3, 2, 8, X),
            vm(3, 2, 8, X),
            vm(3, 2, 8, X),
            vm(3, 2, 8, X),
            vm(RC, 8, X),
            dma(2),
            dma(2, LT),
            dma(4, CH),
            dma(2, CH),
            dma(STEPS),
            dma(STEPS),
            dma(2),
            dma(2),
            dma(2, 5),
            dma(1),
            dma(2),
            dma(8),
            dma(1),
            dma(8),
            dma(2),
            dma(3, 4),
            dma(3, 4),
            dma(4, 2),
            dma(1),
        ],
        compiler_params=pltpu.CompilerParams(
            collective_id=0, has_side_effects=True, vmem_limit_bytes=60 * 2**20
        ),
    )(initial, iterate, diffusivity)
    return pl.pallas_call(
        final_kernel,
        out_shape=jax.ShapeDtypeStruct(iterate.shape, F32),
        in_specs=[hbm, vmem],
        out_specs=hbm,
        scratch_shapes=[vm(LT, 4, Y, 128), vm(LT, 4, Y, 128), dma(LT), dma(LT)],
        compiler_params=pltpu.CompilerParams(vmem_limit_bytes=16 * 2**20),
    )(iterate, err)


def solution(mesh):
    placed = (P("space", None, None), P("tm", "space", None, None), P("space", None, None))
    return jax.shard_map(
        local, mesh=mesh, in_specs=placed, out_specs=P("tm", "space", None, None), check_vma=False
    )
```

```python
import jax
import jax.numpy as jnp
from jax import lax
from jax.experimental import pallas as pl
from jax.experimental.pallas import tpu as pltpu
from jax.sharding import PartitionSpec as P

STEPS = 4
courant = 0.15
K = 0.5 * courant
F32 = jnp.float32
MESH = pl.DeviceIdType.MESH

Y, X = 256, 512
LT = X // 128
R = 32
RC = 16
CH = 12
PART = 8


def lane():
    return lax.broadcasted_iota(jnp.int32, (8, 128), 1)


def even():
    return (lane() & 1) == 0


def subs(shape):
    return lax.broadcasted_iota(jnp.int32, shape, 0)


def from_below(v):
    return jnp.where(subs(v.shape) == 7, 0.0, pltpu.roll(v, 7, axis=0))


def from_above(v):
    return jnp.where(subs(v.shape) == 0, 0.0, pltpu.roll(v, 1, axis=0))


def row(ref, *at):
    return [ref[(*at, slice(None), slice(128 * q, 128 * q + 128))] for q in range(LT)]


def put(ref, value, *at):
    for q in range(LT):
        ref[(*at, slice(None), slice(128 * q, 128 * q + 128))] = value[q]


def each(f, *rows):
    return [f(*t) for t in zip(*rows)]


def add(a, b):
    return each(lambda x, y: x + y, a, b)


def sub(a, b):
    return each(lambda x, y: x - y, a, b)


def mul(a, b):
    return each(lambda x, y: x * y, a, b)


def at_right(v, by=1):
    turned = [pltpu.roll(x, 128 - by, axis=1) for x in v] + [jnp.zeros((8, 128), F32)]
    return [jnp.where(lane() >= 128 - by, turned[q + 1], turned[q]) for q in range(LT)]


def at_left(v, by=1, first=None):
    turned = [jnp.zeros((8, 128), F32) if first is None else first] + [pltpu.roll(x, by, axis=1) for x in v]
    return [jnp.where(lane() < by, turned[q], turned[q + 1]) for q in range(LT)]


def swap_pairs(v):
    return [jnp.where(even(), pltpu.roll(x, 127, axis=1), pltpu.roll(x, 1, axis=1)) for x in v]


def pack(a, b):
    return each(
        lambda x, y: jnp.where(even(), x + pltpu.roll(x, 127, axis=1), y + pltpu.roll(y, 1, axis=1)), a, b
    )


def coarse_advance(c, c_up, c_dn, c_io, v, v_up, v_dn, v_io):
    flux = None
    for cn, vn in (
        (at_right(c, 2), at_right(v, 2)),
        (at_left(c, 2), at_left(v, 2)),
        (c_up, v_up),
        (c_dn, v_dn),
        (swap_pairs(c), swap_pairs(v)),
        (c_io, v_io),
    ):
        term = mul(add(c, cn), sub(vn, v))
        flux = term if flux is None else add(flux, term)
    return each(lambda x, f: x + K * f, v, flux)


def main_kernel(
    ini,
    itr,
    dif,
    out,
    cbuf,
    kx,
    ky,
    kz,
    kl,
    wa,
    wb,
    inn,
    cc,
    ccp,
    icoarse,
    ipart,
    own,
    ext,
    ccb,
    cco,
    go,
    gx,
    eb,
    hlo,
    hhi,
    hp,
    hn,
    eout,
    ld_sem,
    icp,
    chs,
    chr_,
    ins,
    inr,
    pps,
    ppr,
    cbs,
    cbr,
    cor,
    gos,
    gor,
    gxs,
    gxr,
    hs,
    hr,
    eos,
    eor,
):
    t = lax.axis_index("tm")
    s = lax.axis_index("space")
    core = s % 2
    zhi = (s // 2) % 2
    col = s // 4
    z = zhi * 4 + t
    ncol = lax.axis_size("space") // 4
    partner = s + 1 - 2 * core
    cross_ok = jnp.logical_and(
        jnp.logical_or(core == 1, s > 0), jnp.logical_or(core == 0, s < 4 * ncol - 1)
    )
    cross = jnp.where(cross_ok, s - 1 + 2 * core, s)
    qcol = cross // 4
    qzhi = (cross // 2) % 2
    qcore = cross % 2

    states = (wa, wb)

    def plane(p):
        return (3 - p) + core * (2 * p - 3)

    def dev(tt, ss):
        return {"tm": tt, "space": ss}

    barrier = pltpu.get_barrier_semaphore()

    @pl.loop(0, 16)
    def _(i):
        ti, si = i % 4, col * 4 + i // 4

        @pl.when(jnp.logical_not(jnp.logical_and(ti == t, si == s)))
        def _():
            pl.semaphore_signal(barrier, inc=1, device_id=dev(ti, si), device_id_type=MESH)

    lat_ok = jnp.logical_or(
        jnp.logical_and(core == 0, col > 0), jnp.logical_and(core == 1, col < ncol - 1)
    )
    lat_col = jnp.where(core == 0, col - 1, col + 1)

    @pl.when(lat_ok)
    def _():
        @pl.loop(0, 8)
        def _(i):
            si = lat_col * 4 + (i // 4) * 2 + 1 - core
            pl.semaphore_signal(barrier, inc=1, device_id=dev(i % 4, si), device_id_type=MESH)

    def load_rows(src, dst, sem):
        @pl.loop(0, 4)
        def _(p):
            for sl in range(8):
                pltpu.make_async_copy(
                    src.at[plane(p), pl.ds(R * sl, R), :], dst.at[p, pl.ds(1, R), sl, :], sem
                ).start()

    load_rows(dif, cbuf, ld_sem.at[0])

    @pl.when(t == 3)
    def _():
        load_rows(ini, wa, ld_sem.at[1])

    @pl.when(t != 3)
    def _():
        load_rows(itr.at[0], wa, ld_sem.at[1])

    held_c = cbuf.at[pl.ds(0, 4), pl.ds(1, R)]
    pltpu.make_async_copy(held_c, held_c, ld_sem.at[0]).wait()

    pl.semaphore_wait(barrier, jnp.where(lat_ok, 23, 15))

    def inner_c():
        return pltpu.make_async_remote_copy(
            src_ref=cbuf.at[0, pl.ds(1, R)],
            dst_ref=cbuf.at[7, pl.ds(1, R)],
            send_sem=icp.at[0],
            recv_sem=icp.at[1],
            device_id=dev(t, partner),
            device_id_type=MESH,
        )

    inner_c().start()

    def piece(j, ch, i):
        return cbuf.at[j, pl.ds(1 + (R // 2) * ch + (i % 4) * (R // 8), R // 8)]

    def first(ch, i):
        j = i // 4
        return pltpu.make_async_remote_copy(
            src_ref=piece(3 - j, ch, i),
            dst_ref=piece(4 + j, ch, i),
            send_sem=chs.at[2 + ch, i],
            recv_sem=chr_.at[ch, i],
            device_id=dev(3 - 3 * ch, cross),
            device_id_type=MESH,
        )

    def relay(ch, i):
        ref = piece(4 + i // 4, ch, i)
        return pltpu.make_async_remote_copy(
            src_ref=ref,
            dst_ref=ref,
            send_sem=chs.at[ch, i],
            recv_sem=chr_.at[ch, i],
            device_id=dev(jnp.clip(t - 1 + 2 * ch, 0, 3), s),
            device_id_type=MESH,
        )

    starts = (t == 0, t == 3)
    sends_on = (t > 0, t < 3)

    @pl.when(cross_ok)
    def _():
        for ch in range(2):

            @pl.when(starts[ch])
            def _():
                @pl.loop(0, CH)
                def _(i):
                    first(ch, i).start()

    def edge_rows(dst, d):
        dst[d, 0] = from_above(dst[d, R])
        dst[d, R + 1] = from_below(dst[d, 1])

    held_u = wa.at[pl.ds(0, 4), pl.ds(1, R)]
    pltpu.make_async_copy(held_u, held_u, ld_sem.at[1]).wait()

    def inner_state(k):
        return pltpu.make_async_remote_copy(
            src_ref=states[k % 2].at[0, pl.ds(1, R)],
            dst_ref=inn.at[k],
            send_sem=ins.at[k],
            recv_sem=inr.at[k],
            device_id=dev(t, partner),
            device_id_type=MESH,
        )

    inner_state(0).start()
    for p in range(4):
        edge_rows(wa, p)
        edge_rows(cbuf, p)

    def to_partner(i):
        src, dst = ((cc, ccp), (icoarse, ipart))[i]
        return pltpu.make_async_remote_copy(
            src_ref=src,
            dst_ref=dst,
            send_sem=pps.at[i],
            recv_sem=ppr.at[i],
            device_id=dev(t, partner),
            device_id_type=MESH,
        )

    def cross_send(is_self, src, dst, ssem, rsem, to):
        @pl.when(is_self)
        def _():
            pltpu.make_async_copy(src, dst, rsem).start()

        @pl.when(jnp.logical_not(is_self))
        def _():
            pltpu.make_async_remote_copy(
                src_ref=src,
                dst_ref=dst,
                send_sem=ssem,
                recv_sem=rsem,
                device_id=to,
                device_id_type=MESH,
            ).start()

    def cross_sent(is_self, src, dst, ssem, rsem, to):
        @pl.when(jnp.logical_not(is_self))
        def _():
            pltpu.make_async_remote_copy(
                src_ref=src,
                dst_ref=dst,
                send_sem=ssem,
                recv_sem=rsem,
                device_id=to,
                device_id_type=MESH,
            ).wait_send()

    def cc_own(h, m):
        e = t + 4 * h
        sp = col * 4 + h * 2 + zhi
        row = (2 * e - 1 + m + RC) % RC
        return sp == s, cc.at[row], ccb.at[core, m], cbs.at[h, m], cbr.at[0], dev(t, sp)

    def cc_out(h):
        e = t + 4 * h
        sp = qcol * 4 + h * 2 + qzhi
        return sp == s, cc.at[pl.ds(2 * e, 2)], cco.at[qcore], cbs.at[h, 4], cor.at[qcore], dev(t, sp)

    vflag = jnp.where(cross_ok, 1.0, 0.0).astype(F32)

    def coefficients(p):
        @pl.loop(0, R, unroll=4)
        def _(r):
            c = row(cbuf, p, r + 1)
            face = lambda n: each(lambda x, y: K * (x + y), c, n)
            put(kx, face(at_right(c)), p, r)
            put(ky, face(row(cbuf, p, r)), p, r)
            put(kz, face(row(cbuf, (p + 7) % 8, r + 1)), p, r)
            kl[p, r] = K * c[0]

        ky[p, R] = K * (cbuf[p, R] + cbuf[p, R + 1])

    def flux(coeff, a, b):
        return mul(coeff, sub(a, b))

    def step_inner(k):
        inner_state(k).wait_recv()
        src, dst = states[k % 2], states[(k + 1) % 2]
        if k > 0:
            inner_state(k - 1).wait_send()
        step_planes(k, src, dst, 0, 0)
        edge_rows(dst, 0)
        inner_state(k + 1).start()

    def step_rest(k, first, last):
        src, dst = states[k % 2], states[(k + 1) % 2]
        step_planes(k, src, dst, first, last)
        for p in range(first, last + 1 + (last == 3 + k)):
            edge_rows(dst, p)

    def step_planes(k, src, dst, first, last):
        top = 3 + k

        @pl.loop(0, R // 2, unroll=2)
        def _(i):
            r = 2 * i
            below = [row(inn, k, r + j) if first == 0 else row(src, first - 1, r + j + 1) for j in range(2)]
            v = [row(src, first, r + j + 1) for j in range(2)]
            fz = [flux(row(kz, first, r + j), v[j], below[j]) for j in range(2)]
            for p in range(first, last + 1):
                above = None
                if p < top:
                    above = [row(src, p + 1, r + j + 1) for j in range(2)]
                around = [row(src, p, r)] + v + [row(src, p, r + 3)]
                fy = [flux(row(ky, p, r + j), around[j + 1], around[j]) for j in range(3)]
                fz_next = []
                for j in range(2):
                    fx = flux(row(kx, p, r + j), at_right(v[j]), v[j])
                    total = sub(fx, at_left(fx, 1, kl[p, r + j] * v[j][0]))
                    total = add(total, sub(fy[j + 1], fy[j]))
                    if above is None:
                        out_flow = mul(row(kz, p + 1, r + j), v[j])
                        total = sub(total, add(out_flow, fz[j]))
                        if top == 3:
                            out_flow = [vflag * x for x in out_flow]
                        put(dst, out_flow, p + 1, r + j + 1)
                    else:
                        fz_next.append(flux(row(kz, p + 1, r + j), above[j], v[j]))
                        total = add(total, sub(fz_next[j], fz[j]))
                    new = add(v[j], total)
                    if p == 4:
                        new = [vflag * x for x in new]
                    put(dst, new, p, r + j + 1)
                v, fz = above, fz_next

    def restricted():
        @pl.loop(0, RC, unroll=2)
        def _(r):
            def block(src, p):
                a = 2 * r + 1
                return add(add(row(src, p, a), row(src, p, a + 1)), add(row(src, p + 1, a), row(src, p + 1, a + 1)))

            put(cc, [0.125 * x for x in pack(block(cbuf, 0), block(cbuf, 2))], r)
            put(icoarse, [0.125 * x for x in pack(block(wa, 0), block(wa, 2))], r)

    def own_first():
        inner_c().wait_recv()
        edge_rows(cbuf, 7)
        coefficients(0)

    def share_coarse():
        to_partner(0).start()
        to_partner(1).start()
        for h in range(2):
            for m in range(4):
                cross_send(*cc_own(h, m))

            @pl.when(cross_ok)
            def _():
                cross_send(*cc_out(h))

    def after_plane(p, then=None):
        edge_rows(cbuf, p)
        coefficients(p)
        if then is not None:
            then(p - 4)

    early = (restricted, own_first, lambda: coefficients(1), lambda: coefficients(2), lambda: coefficients(3))
    late = (
        lambda: after_plane(4),
        lambda: step_inner(0),
        lambda: step_rest(0, 1, 3),
        share_coarse,
        lambda: after_plane(5, step_inner),
        lambda: step_rest(1, 1, 4),
        lambda: step_inner(2),
        lambda: step_rest(2, 1, 4),
    )

    off = tuple(
        jnp.where(t == last, 7, jnp.where(t == near, 3, 0)) for last, near in ((0, 1), (3, 2))
    )
    off_max = jnp.maximum(off[0], off[1])

    @pl.when(jnp.logical_not(cross_ok))
    def _():
        for p in range(4, 7):

            @pl.loop(0, R + 2)
            def _(r):
                cbuf[p, r] = jnp.zeros((8, X), F32)

    @pl.loop(0, CH + 7)
    def _(n):
        for ch in range(2):
            i = n - off[ch]

            @pl.when(jnp.logical_and(cross_ok, jnp.logical_and(i >= 0, i < CH)))
            def _():
                relay(ch, i).wait_recv()

                @pl.when(sends_on[ch])
                def _():
                    relay(ch, i).start()

        for m, work in enumerate(early):
            pl.when(n == m)(work)
        for m, work in enumerate(late):
            pl.when(n == 3 + off_max + m)(work)

    to_partner(0).wait_recv()
    to_partner(1).wait_recv()
    gflag = jnp.where(t == 3, 0.0, 1.0).astype(F32)
    inner_state(STEPS - 1).wait_recv()

    def last_groups(r, groups, low):
        src = states[(STEPS - 1) % 2]
        ends = []
        v = [row(src, groups[0][0], r + j + 1) for j in range(2)]
        low = [flux(row(kz, groups[0][0], r + j), v[j], low(j)) for j in range(2)]
        low = add(low[0], low[1])
        for planes in groups:
            held = fxs = net = kls = None
            for p in planes:
                fy = sub(
                    flux(row(ky, p, r + 2), row(src, p, r + 3), v[1]), flux(row(ky, p, r), v[0], row(src, p, r))
                )
                net = fy if net is None else add(net, fy)
                for j in range(2):
                    fx = flux(row(kx, p, r + j), at_right(v[j]), v[j])
                    fl = kl[p, r + j] * v[j][0]
                    fxs = fx if fxs is None else add(fxs, fx)
                    kls = fl if kls is None else kls + fl
                both = add(v[0], v[1])
                held = both if held is None else add(held, both)
                if p < 6:
                    last_v, v = v, [row(src, p + 1, r + j + 1) for j in range(2)]
            net = sub(net, low)
            if planes[-1] < 6:
                high = [flux(row(kz, planes[-1] + 1, r + j), v[j], last_v[j]) for j in range(2)]
                low = add(high[0], high[1])
                net = add(net, low)
            held = add(held, net)
            right = [pltpu.roll(x, 127, axis=1) for x in add(held, fxs)]
            ends.append(sub(add(held, right), at_left(fxs, 1, kls)))
        return ends

    def packed(a, b):
        return each(lambda x, y: 0.125 * jnp.where(even(), x, pltpu.roll(y, 1, axis=1)), a, b)

    def coarse_side(rc):
        a = 2 * rc + 1
        outer = add(add(row(cbuf, 4, a), row(cbuf, 4, a + 1)), add(row(cbuf, 5, a), row(cbuf, 5, a + 1)))
        return each(lambda x, y: jnp.where(even(), x, 0.125 * y), row(ccp, rc), pack(outer, outer))

    def own_row(rc):
        lo = jnp.maximum(rc - 1, 0)
        hi = jnp.minimum(rc + 1, RC - 1)

        def neighbours(ref):
            up = each(lambda x, y: jnp.where(rc == RC - 1, from_below(y), x), row(ref, hi), row(ref, 0))
            dn = each(lambda x, y: jnp.where(rc == 0, from_above(y), x), row(ref, lo), row(ref, RC - 1))
            return up, dn

        ends = last_groups(2 * rc, ((0, 1), (2, 3)), lambda j: row(inn, STEPS - 1, 2 * rc + j))
        c_up, c_dn = neighbours(cc)
        u_up, u_dn = neighbours(icoarse)
        u_io = [jnp.where(even(), x, 0.0) for x in row(ipart, rc)]
        back = coarse_advance(
            row(cc, rc), c_up, c_dn, coarse_side(rc), row(icoarse, rc), u_up, u_dn, u_io
        )
        put(own, each(lambda x, y: x - gflag * y, packed(ends[0], ends[1]), back), rc)

    def ext_row(rc):
        src = states[(STEPS - 1) % 2]
        ends = last_groups(2 * rc, ((4, 5), (6,)), lambda j: row(src, 3, 2 * rc + j + 1))
        lost = each(
            lambda x, y, z: jnp.where(even(), 0.0, K * (x + y) * z),
            row(cc, rc),
            coarse_side(rc),
            row(icoarse, rc),
        )
        put(ext, each(lambda x, y: x - gflag * y, packed(ends[1], ends[0]), lost), rc)

    def o_send(e):
        sp = col * 4 + (e // 4) * 2 + zhi
        te = e % 4
        return (
            jnp.logical_and(sp == s, te == t),
            own.at[pl.ds(2 * e, 2)],
            go.at[t, core],
            gos.at[e],
            gor.at[0],
            dev(te, sp),
        )

    def x_send(e):
        sp = qcol * 4 + (e // 4) * 2 + qzhi
        te = e % 4
        return (
            jnp.logical_and(sp == s, te == t),
            ext.at[pl.ds(2 * e, 2)],
            gx.at[qcore, t],
            gxs.at[e],
            gxr.at[qcore],
            dev(te, sp),
        )

    def rows_and_sends(one_row, send):
        @pl.loop(0, 9)
        def _(i):
            @pl.when(i < 8)
            def _():
                e = (z + 4 + i) % 8
                one_row(2 * e)
                one_row(2 * e + 1)

            @pl.when(i > 0)
            def _():
                cross_send(*send((z + 3 + i) % 8))

    rows_and_sends(own_row, o_send)
    after_plane(6)
    step_rest(2, 5, 5)

    @pl.when(cross_ok)
    def _():
        rows_and_sends(ext_row, x_send)

    prev_ok = jnp.logical_or(core == 1, col > 0)
    next_ok = jnp.logical_or(core == 0, col < ncol - 1)
    prev_sp = jnp.where(core == 1, s - 1, jnp.maximum(col - 1, 0) * 4 + zhi * 2 + 1)
    next_sp = jnp.where(core == 0, s + 1, jnp.minimum(col + 1, ncol - 1) * 4 + zhi * 2)
    side_ok = (prev_ok, next_ok)

    pltpu.make_async_copy(ccb, ccb, cbr.at[0]).wait()
    for j in range(2):

        @pl.when(side_ok[j])
        def _():
            pltpu.make_async_copy(cco.at[j], cco.at[j], cor.at[j]).wait()

        @pl.when(jnp.logical_not(side_ok[j]))
        def _():
            cco[j] = jnp.zeros((2, 8, X), F32)
            gx[j] = jnp.zeros((4, 2, 8, X), F32)

    pltpu.make_async_copy(go, go, gor.at[0]).wait()
    for j in range(2):

        @pl.when(side_ok[j])
        def _():
            pltpu.make_async_copy(gx.at[j], gx.at[j], gxr.at[j]).wait()

    zu, zd = (z + 1) % 8, (z + 7) % 8

    def e_halo(k, kind):
        if kind == 0:
            src, dst, to = eb.at[k, 0], hhi.at[k], dev(zd % 4, col * 4 + (zd // 4) * 2 + core)
        elif kind == 1:
            src, dst, to = eb.at[k, 1], hlo.at[k], dev(zu % 4, col * 4 + (zu // 4) * 2 + core)
        elif kind == 2:
            src, dst, to = eb.at[k, :, 0], hn.at[k], dev(t, prev_sp)
        else:
            src, dst, to = eb.at[k, :, 1], hp.at[k], dev(t, next_sp)
        return pltpu.make_async_remote_copy(
            src_ref=src,
            dst_ref=dst,
            send_sem=hs.at[k, kind],
            recv_sem=hr.at[k, kind],
            device_id=to,
            device_id_type=MESH,
        )

    def e_back(k, j):
        sp = col * 4 + core * 2 + j
        return (
            jnp.logical_and(sp == s, t == k),
            eb.at[k, :, j],
            eout.at[pl.ds(2 * z, 2)],
            eos.at[k, j],
            eor.at[0],
            dev(k, sp),
        )

    for b in range(2):
        for j in range(2):
            eb[0, b, j] = go[3, j, b] + gx[j, 3, b]

    def send_level(k):
        if k < 3:
            e_halo(k, 0).start()
            e_halo(k, 1).start()

            @pl.when(prev_ok)
            def _():
                e_halo(k, 2).start()

            @pl.when(next_ok)
            def _():
                e_halo(k, 3).start()

        for j in range(2):
            cross_send(*e_back(k, j))

    send_level(0)
    for k in range(3):
        e_halo(k, 0).wait_recv()
        e_halo(k, 1).wait_recv()

        @pl.when(next_ok)
        def _():
            e_halo(k, 2).wait_recv()

        @pl.when(prev_ok)
        def _():
            e_halo(k, 3).wait_recv()

        @pl.when(jnp.logical_not(next_ok))
        def _():
            hn[k] = jnp.zeros((2, 8, X), F32)

        @pl.when(jnp.logical_not(prev_ok))
        def _():
            hp[k] = jnp.zeros((2, 8, X), F32)

        for j in range(2):

            def wrapped(x, c, turn, at_end):
                return [jnp.where(at_end, turn(y), y) for y in row(x, *c)]

            vs = (
                wrapped(hlo, (k, j), from_above, z == 0),
                row(eb, k, 0, j),
                row(eb, k, 1, j),
                wrapped(hhi, (k, j), from_below, z == 7),
            )
            cs = (
                wrapped(ccb, (j, 0), from_above, z == 0),
                row(ccb, j, 1),
                row(ccb, j, 2),
                wrapped(ccb, (j, 3), from_below, z == 7),
            )
            for b in range(2):
                far = row(hp if j == 0 else hn, k, b)
                v_io = each(lambda x, y: jnp.where(even(), x, y), row(eb, k, b, 1 - j), far)
                c_io = each(lambda x, y: jnp.where(even(), x, y), row(ccb, 1 - j, b + 1), row(cco, j, b))
                new = coarse_advance(
                    cs[b + 1], cs[b + 2], cs[b], c_io, vs[b + 1], vs[b + 2], vs[b], v_io
                )
                put(eb, add(new, add(row(go, k, j, b), row(gx, j, k, b))), k + 1, b, j)
        send_level(k + 1)

    pltpu.make_async_copy(eout, eout, eor.at[0]).wait()
    result = pltpu.make_async_copy(eout, out, ld_sem.at[0])
    result.start()

    inner_c().wait_send()
    for k in range(STEPS - 2, STEPS):
        inner_state(k).wait_send()
    for i in range(2):
        to_partner(i).wait_send()

    @pl.when(cross_ok)
    def _():
        for ch in range(2):

            @pl.when(starts[ch])
            def _():
                @pl.loop(0, CH)
                def _(i):
                    first(ch, i).wait_send()

            @pl.when(sends_on[ch])
            def _():
                @pl.loop(0, CH)
                def _(i):
                    relay(ch, i).wait_send()

    for h in range(2):
        for m in range(4):
            cross_sent(*cc_own(h, m))

        @pl.when(cross_ok)
        def _():
            cross_sent(*cc_out(h))

    @pl.loop(0, 8)
    def _(e):
        cross_sent(*o_send(e))

        @pl.when(cross_ok)
        def _():
            cross_sent(*x_send(e))

    for k in range(3):
        e_halo(k, 0).wait_send()
        e_halo(k, 1).wait_send()

        @pl.when(prev_ok)
        def _():
            e_halo(k, 2).wait_send()

        @pl.when(next_ok)
        def _():
            e_halo(k, 3).wait_send()

    for k in range(4):
        for j in range(2):
            cross_sent(*e_back(k, j))
    result.wait()


def final_kernel(itr, err, out, e, raw, res, esem, isem, osem):
    core = lax.axis_index("space") % 2

    def plane(p):
        return (3 - p) + core * (2 * p - 3)

    def load(n, sl):
        return pltpu.make_async_copy(
            itr.at[0, :, pl.ds(R * sl + PART * n, PART), :], raw.at[n, :, :, sl, :], isem.at[n]
        )

    def store(n, sl):
        return pltpu.make_async_copy(
            res.at[n, :, :, sl, :], out.at[0, :, pl.ds(R * sl + PART * n, PART), :], osem.at[n]
        )

    fetch = pltpu.make_async_copy(err, e, esem.at[0])
    fetch.start()
    for n in range(R // PART):
        for sl in range(8):
            load(n, sl).start()
    fetch.wait()
    for n in range(R // PART):
        pltpu.make_async_copy(raw.at[n], raw.at[n], isem.at[n]).wait()

        @pl.loop(0, PART // 2, unroll=2)
        def _(r):
            rows = [[row(raw, n, plane(p), 2 * r + b) for b in range(2)] for p in range(4)]
            a = add(add(*rows[0]), add(*rows[1]))
            c = add(add(*rows[2]), add(*rows[3]))
            d = each(lambda x, y: x - 0.125 * y, row(e, (PART // 2) * n + r), pack(a, c))
            halves = (
                [jnp.where(even(), x, pltpu.roll(x, 1, axis=1)) for x in d],
                [jnp.where(even(), pltpu.roll(x, 127, axis=1), x) for x in d],
            )
            for p in range(4):
                for b in range(2):
                    put(res, add(rows[p][b], halves[p // 2]), n, plane(p), 2 * r + b)

        for sl in range(8):
            store(n, sl).start()
    for n in range(R // PART):
        pltpu.make_async_copy(res.at[n], res.at[n], osem.at[n]).wait()


def local(initial, iterate, diffusivity):
    vm = lambda *shape: pltpu.VMEM(shape, F32)
    dma = lambda *shape: pltpu.SemaphoreType.DMA(shape)
    hbm = pl.BlockSpec(memory_space=pl.ANY)
    err = pl.pallas_call(
        main_kernel,
        out_shape=jax.ShapeDtypeStruct((RC, 8, X), F32),
        in_specs=[hbm] * 3,
        out_specs=hbm,
        scratch_shapes=[
            vm(8, R + 2, 8, X),
            vm(7, R, 8, X),
            vm(7, R + 1, 8, X),
            vm(7, R, 8, X),
            vm(7, R, 8, 128),
            vm(7, R + 2, 8, X),
            vm(7, R + 2, 8, X),
            vm(STEPS, R, 8, X),
            vm(RC, 8, X),
            vm(RC, 8, X),
            vm(RC, 8, X),
            vm(RC, 8, X),
            vm(RC, 8, X),
            vm(RC, 8, X),
            vm(2, 4, 8, X),
            vm(2, 2, 8, X),
            vm(4, 2, 2, 8, X),
            vm(2, 4, 2, 8, X),
            vm(4, 2, 2, 8, X),
            vm(3, 2, 8, X),
            vm(3, 2, 8, X),
            vm(3, 2, 8, X),
            vm(3, 2, 8, X),
            vm(RC, 8, X),
            dma(2),
            dma(2),
            dma(4, CH),
            dma(2, CH),
            dma(STEPS),
            dma(STEPS),
            dma(2),
            dma(2),
            dma(2, 5),
            dma(1),
            dma(2),
            dma(8),
            dma(1),
            dma(8),
            dma(2),
            dma(3, 4),
            dma(3, 4),
            dma(4, 2),
            dma(1),
        ],
        compiler_params=pltpu.CompilerParams(
            collective_id=0, has_side_effects=True, vmem_limit_bytes=60 * 2**20
        ),
    )(initial, iterate, diffusivity)
    return pl.pallas_call(
        final_kernel,
        out_shape=jax.ShapeDtypeStruct(iterate.shape, F32),
        in_specs=[hbm, hbm],
        out_specs=hbm,
        scratch_shapes=[
            vm(RC, 8, X),
            vm(R // PART, 4, PART, 8, X),
            vm(R // PART, 4, PART, 8, X),
            dma(1),
            dma(R // PART),
            dma(R // PART),
        ],
        compiler_params=pltpu.CompilerParams(vmem_limit_bytes=16 * 2**20),
    )(iterate, err)


def solution(mesh):
    placed = (P("space", None, None), P("tm", "space", None, None), P("space", None, None))
    return jax.shard_map(
        local, mesh=mesh, in_specs=placed, out_specs=P("tm", "space", None, None), check_vma=False
    )
```

```python
import functools

import jax
import jax.numpy as jnp
from jax import lax
from jax.experimental import pallas as pl
from jax.experimental.pallas import tpu as pltpu
from jax.sharding import PartitionSpec as P

STEPS = 4
courant = 0.15
K = 0.5 * courant
F32 = jnp.float32
MESH = pl.DeviceIdType.MESH

Y, X = 256, 512
LT = X // 128
R = 32
RC = 16
CH = 24
LEAD, FAR = 5, 14
PART = 64


PER = CH // 3


def lane():
    return lax.broadcasted_iota(jnp.int32, (8, 128), 1)


def even():
    return (lane() & 1) == 0


def subs(shape):
    return lax.broadcasted_iota(jnp.int32, shape, 0)


def from_below(v):
    return jnp.where(subs(v.shape) == 7, 0.0, pltpu.roll(v, 7, axis=0))


def from_above(v):
    return jnp.where(subs(v.shape) == 0, 0.0, pltpu.roll(v, 1, axis=0))


def row(ref, *at):
    return [ref[(*at, slice(None), slice(128 * q, 128 * q + 128))] for q in range(LT)]


def put(ref, value, *at):
    for q in range(LT):
        ref[(*at, slice(None), slice(128 * q, 128 * q + 128))] = value[q]


def each(f, *rows):
    return [f(*t) for t in zip(*rows)]


def add(a, b):
    return each(lambda x, y: x + y, a, b)


def sub(a, b):
    return each(lambda x, y: x - y, a, b)


def mul(a, b):
    return each(lambda x, y: x * y, a, b)


def at_right(v, by=1):
    turned = [pltpu.roll(x, 128 - by, axis=1) for x in v] + [jnp.zeros((8, 128), F32)]
    return [jnp.where(lane() >= 128 - by, turned[q + 1], turned[q]) for q in range(LT)]


def at_left(v, by=1, first=None):
    turned = [jnp.zeros((8, 128), F32) if first is None else first] + [pltpu.roll(x, by, axis=1) for x in v]
    return [jnp.where(lane() < by, turned[q], turned[q + 1]) for q in range(LT)]


def swap_pairs(v):
    return [jnp.where(even(), pltpu.roll(x, 127, axis=1), pltpu.roll(x, 1, axis=1)) for x in v]


def pack(a, b):
    return each(
        lambda x, y: jnp.where(even(), x + pltpu.roll(x, 127, axis=1), y + pltpu.roll(y, 1, axis=1)), a, b
    )


def coarse_advance(c, c_up, c_dn, c_io, v, v_up, v_dn, v_io):
    flux = None
    for cn, vn in (
        (at_right(c, 2), at_right(v, 2)),
        (at_left(c, 2), at_left(v, 2)),
        (c_up, v_up),
        (c_dn, v_dn),
        (swap_pairs(c), swap_pairs(v)),
        (c_io, v_io),
    ):
        term = mul(add(c, cn), sub(vn, v))
        flux = term if flux is None else add(flux, term)
    return each(lambda x, f: x + K * f, v, flux)


def main_kernel(
    ini,
    itr,
    dif,
    out,
    cbuf,
    kx,
    ky,
    kz,
    kl,
    wa,
    wb,
    inn,
    cc,
    ccp,
    icoarse,
    ipart,
    own,
    ext,
    ccb,
    cco,
    go,
    gx,
    eb,
    hlo,
    hhi,
    hp,
    hn,
    eout,
    wide,
    ld_sem,
    icp,
    chs,
    chr_,
    ins,
    inr,
    pps,
    ppr,
    cbs,
    cbr,
    cos,
    cor,
    gos,
    gor,
    gxs,
    gxr,
    hs,
    hr,
    eos,
    eor,
):
    t = lax.axis_index("tm")
    s = lax.axis_index("space")
    core = s % 2
    zhi = (s // 2) % 2
    col = s // 4
    z = zhi * 4 + t
    ncol = lax.axis_size("space") // 4
    partner = s + 1 - 2 * core
    cross_ok = jnp.logical_and(
        jnp.logical_or(core == 1, s > 0), jnp.logical_or(core == 0, s < 4 * ncol - 1)
    )
    cross = jnp.where(cross_ok, s - 1 + 2 * core, s)
    qcol = cross // 4
    qzhi = (cross // 2) % 2
    qcore = cross % 2

    states = (wa, wb)

    def plane(p):
        return (3 - p) + core * (2 * p - 3)

    def dev(tt, ss):
        return {"tm": tt, "space": ss}

    barrier = pltpu.get_barrier_semaphore()

    @pl.loop(0, 16)
    def _(i):
        ti, si = i % 4, col * 4 + i // 4

        @pl.when(jnp.logical_not(jnp.logical_and(ti == t, si == s)))
        def _():
            pl.semaphore_signal(barrier, inc=1, device_id=dev(ti, si), device_id_type=MESH)

    lat_ok = jnp.logical_or(
        jnp.logical_and(core == 0, col > 0), jnp.logical_and(core == 1, col < ncol - 1)
    )
    lat_col = jnp.where(core == 0, col - 1, col + 1)

    @pl.when(lat_ok)
    def _():
        @pl.loop(0, 8)
        def _(i):
            si = lat_col * 4 + (i // 4) * 2 + 1 - core
            pl.semaphore_signal(barrier, inc=1, device_id=dev(i % 4, si), device_id_type=MESH)

    def load_rows(src, dst, sem):
        @pl.loop(0, 4)
        def _(p):
            for sl in range(8):
                pltpu.make_async_copy(
                    src.at[plane(p), pl.ds(R * sl, R), :], dst.at[p, pl.ds(1, R), sl, :], sem
                ).start()

    load_rows(dif, cbuf, ld_sem.at[0])

    @pl.when(t == 3)
    def _():
        load_rows(ini, wa, ld_sem.at[1])

    @pl.when(t != 3)
    def _():
        load_rows(itr.at[0], wa, ld_sem.at[1])

    held_c = cbuf.at[pl.ds(0, 4), pl.ds(1, R)]
    pltpu.make_async_copy(held_c, held_c, ld_sem.at[0]).wait()

    pl.semaphore_wait(barrier, jnp.where(lat_ok, 23, 15))

    def inner_c():
        return pltpu.make_async_remote_copy(
            src_ref=cbuf.at[0, pl.ds(1, R)],
            dst_ref=cbuf.at[7, pl.ds(1, R)],
            send_sem=icp.at[0],
            recv_sem=icp.at[1],
            device_id=dev(t, partner),
            device_id_type=MESH,
        )

    inner_c().start()

    def piece(j, ch, i):
        return cbuf.at[j, pl.ds(1 + (R // 2) * ch + (i % PER) * (R // 2 // PER), R // 2 // PER)]

    def first(ch, i):
        j = i // PER
        return pltpu.make_async_remote_copy(
            src_ref=piece(3 - j, ch, i),
            dst_ref=piece(4 + j, ch, i),
            send_sem=chs.at[2 + ch, i],
            recv_sem=chr_.at[ch, i],
            device_id=dev(3 - 3 * ch, cross),
            device_id_type=MESH,
        )

    def relay(ch, i):
        ref = piece(4 + i // PER, ch, i)
        return pltpu.make_async_remote_copy(
            src_ref=ref,
            dst_ref=ref,
            send_sem=chs.at[ch, i],
            recv_sem=chr_.at[ch, i],
            device_id=dev(jnp.clip(t - 1 + 2 * ch, 0, 3), s),
            device_id_type=MESH,
        )

    starts = (t == 0, t == 3)
    sends_on = (t > 0, t < 3)

    @pl.when(cross_ok)
    def _():
        for ch in range(2):

            @pl.when(starts[ch])
            def _():
                @pl.loop(0, CH)
                def _(i):
                    first(ch, i).start()

    def edge_rows(dst, d):
        dst[d, 0] = from_above(dst[d, R])
        dst[d, R + 1] = from_below(dst[d, 1])

    held_u = wa.at[pl.ds(0, 4), pl.ds(1, R)]
    pltpu.make_async_copy(held_u, held_u, ld_sem.at[1]).wait()

    def inner_state(k):
        return pltpu.make_async_remote_copy(
            src_ref=states[k % 2].at[0, pl.ds(1, R)],
            dst_ref=inn.at[k],
            send_sem=ins.at[k],
            recv_sem=inr.at[k],
            device_id=dev(t, partner),
            device_id_type=MESH,
        )

    inner_state(0).start()
    for p in range(4):
        edge_rows(wa, p)
        edge_rows(cbuf, p)

    def to_partner(i):
        src, dst = ((cc, ccp), (icoarse, ipart))[i]
        return pltpu.make_async_remote_copy(
            src_ref=src,
            dst_ref=dst,
            send_sem=pps.at[i],
            recv_sem=ppr.at[i],
            device_id=dev(t, partner),
            device_id_type=MESH,
        )

    def cross_send(is_self, src, dst, ssem, rsem, to):
        @pl.when(is_self)
        def _():
            pltpu.make_async_copy(src, dst, rsem).start()

        @pl.when(jnp.logical_not(is_self))
        def _():
            pltpu.make_async_remote_copy(
                src_ref=src,
                dst_ref=dst,
                send_sem=ssem,
                recv_sem=rsem,
                device_id=to,
                device_id_type=MESH,
            ).start()

    def cross_sent(is_self, src, dst, ssem, rsem, to):
        @pl.when(jnp.logical_not(is_self))
        def _():
            pltpu.make_async_remote_copy(
                src_ref=src,
                dst_ref=dst,
                send_sem=ssem,
                recv_sem=rsem,
                device_id=to,
                device_id_type=MESH,
            ).wait_send()

    def cc_own(h):
        e = t + 4 * h
        sp = col * 4 + h * 2 + zhi
        return (
            sp == s,
            cc.at[pl.ds(2 * e, 2)],
            ccb.at[core, pl.ds(1, 2)],
            cbs.at[h],
            cbr.at[0],
            dev(t, sp),
        )

    prev_ok = jnp.logical_or(core == 1, col > 0)
    next_ok = jnp.logical_or(core == 0, col < ncol - 1)
    prev_sp = jnp.where(core == 1, s - 1, jnp.maximum(col - 1, 0) * 4 + zhi * 2 + 1)
    next_sp = jnp.where(core == 0, s + 1, jnp.minimum(col + 1, ncol - 1) * 4 + zhi * 2)
    side_ok = (prev_ok, next_ok)

    zu, zd = (z + 1) % 8, (z + 7) % 8
    beside = (
        dev(zd % 4, col * 4 + (zd // 4) * 2 + core),
        dev(zu % 4, col * 4 + (zu // 4) * 2 + core),
        dev(t, prev_sp),
        dev(t, next_sp),
    )

    def c_halo(kind):
        src, dst = (
            (ccb.at[:, 1], ccb.at[:, 3]),
            (ccb.at[:, 2], ccb.at[:, 0]),
            (ccb.at[0, pl.ds(1, 2)], cco.at[1]),
            (ccb.at[1, pl.ds(1, 2)], cco.at[0]),
        )[kind]
        return pltpu.make_async_remote_copy(
            src_ref=src,
            dst_ref=dst,
            send_sem=cos.at[kind],
            recv_sem=cor.at[kind],
            device_id=beside[kind],
            device_id_type=MESH,
        )

    def share_halos():
        held = ccb.at[:, pl.ds(1, 2)]
        pltpu.make_async_copy(held, held, cbr.at[0]).wait()
        c_halo(0).start()
        c_halo(1).start()

        @pl.when(prev_ok)
        def _():
            c_halo(2).start()

        @pl.when(next_ok)
        def _():
            c_halo(3).start()

    vflag = jnp.where(cross_ok, 1.0, 0.0).astype(F32)
    gflag = jnp.where(t == 3, 0.0, 1.0).astype(F32)

    def coefficients(p):
        @pl.loop(0, R, unroll=4)
        def _(r):
            c = row(cbuf, p, r + 1)
            face = lambda n: each(lambda x, y: K * (x + y), c, n)
            put(kx, face(at_right(c)), p, r)
            put(ky, face(row(cbuf, p, r)), p, r)
            put(kz, face(row(cbuf, (p + 7) % 8, r + 1)), p, r)
            kl[p, r] = K * c[0]

        ky[p, R] = K * (cbuf[p, R] + cbuf[p, R + 1])

    def flux(coeff, a, b):
        return mul(coeff, sub(a, b))

    def step_inner(k, lo=0, hi=R // 2):
        src, dst = states[k % 2], states[(k + 1) % 2]
        if lo == 0:
            inner_state(k).wait_recv()
            if k > 0:
                inner_state(k - 1).wait_send()
        step_planes(k, src, dst, 0, 0, lo, hi)
        if hi == R // 2:
            edge_rows(dst, 0)
            inner_state(k + 1).start()

    def step_rest(k, first, last, lo=0, hi=R // 2):
        src, dst = states[k % 2], states[(k + 1) % 2]
        step_planes(k, src, dst, first, last, lo, hi)
        if hi < R // 2:
            return
        for p in range(first, last + 1 + (last == 3 + k)):
            edge_rows(dst, p)

    def step_planes(k, src, dst, first, last, lo, hi):
        top = 3 + k

        @pl.loop(lo, hi, unroll=2)
        def _(i):
            r = 2 * i
            below = [row(inn, k, r + j) if first == 0 else row(src, first - 1, r + j + 1) for j in range(2)]
            v = [row(src, first, r + j + 1) for j in range(2)]
            fz = [flux(row(kz, first, r + j), v[j], below[j]) for j in range(2)]
            for p in range(first, last + 1):
                above = None
                if p < top:
                    above = [row(src, p + 1, r + j + 1) for j in range(2)]
                around = [row(src, p, r)] + v + [row(src, p, r + 3)]
                fy = [flux(row(ky, p, r + j), around[j + 1], around[j]) for j in range(3)]
                fz_next = []
                for j in range(2):
                    fx = flux(row(kx, p, r + j), at_right(v[j]), v[j])
                    total = sub(fx, at_left(fx, 1, kl[p, r + j] * v[j][0]))
                    total = add(total, sub(fy[j + 1], fy[j]))
                    if above is None:
                        out_flow = mul(row(kz, p + 1, r + j), v[j])
                        total = sub(total, add(out_flow, fz[j]))
                        if top == 3:
                            out_flow = [vflag * x for x in out_flow]
                        put(dst, out_flow, p + 1, r + j + 1)
                    else:
                        fz_next.append(flux(row(kz, p + 1, r + j), above[j], v[j]))
                        total = add(total, sub(fz_next[j], fz[j]))
                    new = add(v[j], total)
                    if p == 4:
                        new = [vflag * x for x in new]
                    put(dst, new, p, r + j + 1)
                v, fz = above, fz_next

    def restricted():
        @pl.loop(0, RC, unroll=2)
        def _(r):
            def block(src, p):
                a = 2 * r + 1
                return add(add(row(src, p, a), row(src, p, a + 1)), add(row(src, p + 1, a), row(src, p + 1, a + 1)))

            put(cc, [0.125 * x for x in pack(block(cbuf, 0), block(cbuf, 2))], r)
            put(icoarse, [0.125 * x for x in pack(block(wa, 0), block(wa, 2))], r)

    def own_first():
        inner_c().wait_recv()
        edge_rows(cbuf, 7)
        coefficients(0)

    def share_coarse():
        to_partner(0).start()
        to_partner(1).start()
        for h in range(2):
            cross_send(*cc_own(h))

    def after_plane(p):
        edge_rows(cbuf, p)
        coefficients(p)

    def last_groups(r, groups, low):
        src = states[(STEPS - 1) % 2]
        ends = []
        v = [row(src, groups[0][0], r + j + 1) for j in range(2)]
        low = [flux(row(kz, groups[0][0], r + j), v[j], low(j)) for j in range(2)]
        low = add(low[0], low[1])
        for planes in groups:
            held = fxs = net = kls = None
            for p in planes:
                fy = sub(
                    flux(row(ky, p, r + 2), row(src, p, r + 3), v[1]), flux(row(ky, p, r), v[0], row(src, p, r))
                )
                net = fy if net is None else add(net, fy)
                for j in range(2):
                    fx = flux(row(kx, p, r + j), at_right(v[j]), v[j])
                    fl = kl[p, r + j] * v[j][0]
                    fxs = fx if fxs is None else add(fxs, fx)
                    kls = fl if kls is None else kls + fl
                both = add(v[0], v[1])
                held = both if held is None else add(held, both)
                if p < 6:
                    last_v, v = v, [row(src, p + 1, r + j + 1) for j in range(2)]
            net = sub(net, low)
            if planes[-1] < 6:
                high = [flux(row(kz, planes[-1] + 1, r + j), v[j], last_v[j]) for j in range(2)]
                low = add(high[0], high[1])
                net = add(net, low)
            held = add(held, net)
            right = [pltpu.roll(x, 127, axis=1) for x in add(held, fxs)]
            ends.append(sub(add(held, right), at_left(fxs, 1, kls)))
        return ends

    def packed(a, b):
        return each(lambda x, y: 0.125 * jnp.where(even(), x, pltpu.roll(y, 1, axis=1)), a, b)

    def coarse_side(rc):
        a = 2 * rc + 1
        outer = add(add(row(cbuf, 4, a), row(cbuf, 4, a + 1)), add(row(cbuf, 5, a), row(cbuf, 5, a + 1)))
        return each(lambda x, y: jnp.where(even(), x, 0.125 * y), row(ccp, rc), pack(outer, outer))

    def inner_rows(lo, hi):
        if lo == 0:
            inner_state(STEPS - 1).wait_recv()

        @pl.loop(lo, hi)
        def _(rc):
            put(own, last_groups(2 * rc, ((0, 1),), lambda j: row(inn, STEPS - 1, 2 * rc + j))[0], rc)

    def own_row(rc):
        lo = jnp.maximum(rc - 1, 0)
        hi = jnp.minimum(rc + 1, RC - 1)

        def neighbours(ref):
            up = each(lambda x, y: jnp.where(rc == RC - 1, from_below(y), x), row(ref, hi), row(ref, 0))
            dn = each(lambda x, y: jnp.where(rc == 0, from_above(y), x), row(ref, lo), row(ref, RC - 1))
            return up, dn

        src = states[(STEPS - 1) % 2]
        ends = last_groups(2 * rc, ((2, 3),), lambda j: row(src, 1, 2 * rc + j + 1))
        c_up, c_dn = neighbours(cc)
        u_up, u_dn = neighbours(icoarse)
        u_io = [jnp.where(even(), x, 0.0) for x in row(ipart, rc)]
        back = coarse_advance(
            row(cc, rc), c_up, c_dn, coarse_side(rc), row(icoarse, rc), u_up, u_dn, u_io
        )
        put(own, each(lambda x, y: x - gflag * y, packed(row(own, rc), ends[0]), back), rc)

    def ext_row(rc):
        src = states[(STEPS - 1) % 2]
        ends = last_groups(2 * rc, ((4, 5), (6,)), lambda j: row(src, 3, 2 * rc + j + 1))
        lost = each(
            lambda x, y, z: jnp.where(even(), 0.0, K * (x + y) * z),
            row(cc, rc),
            coarse_side(rc),
            row(icoarse, rc),
        )
        put(ext, each(lambda x, y: x - gflag * y, packed(ends[1], ends[0]), lost), rc)

    def parts(f, *args, n):
        cuts = [R // 2 * i // n for i in range(n + 1)]
        return [functools.partial(f, *args, lo, hi) for lo, hi in zip(cuts, cuts[1:])]

    first_items = [functools.partial(coefficients, p) for p in (1, 2, 3)] + parts(step_inner, 0, n=2)
    items = [
        *parts(step_rest, 0, 1, 2, n=4),
        *parts(step_inner, 1, n=2),
        *parts(step_rest, 1, 1, 1, n=2),
        *parts(step_inner, 2, n=2),
    ]
    items += [None] * (PER - 1 + FAR - len(first_items) - len(items))
    items += [
        functools.partial(after_plane, 4),
        *parts(step_rest, 0, 3, 3, n=2),
        *parts(step_rest, 1, 2, 3, n=4),
        *parts(step_rest, 2, 1, 2, n=4),
        *parts(inner_rows, n=4),
        functools.partial(after_plane, 5),
        *parts(step_rest, 1, 4, 4, n=2),
        *parts(step_rest, 2, 3, 4, n=4),
    ]
    middle = jnp.logical_or(t == 1, t == 2)
    restricted()
    share_coarse()
    own_first()

    @pl.when(middle)
    def _():
        for work in first_items:
            work()

    def on_ends(work):
        return lambda: pl.when(jnp.logical_not(middle))(work)

    items = [on_ends(work) for work in first_items] + items

    off = tuple(
        jnp.where(t == last, FAR, jnp.where(t == near, LEAD, 0)) for last, near in ((0, 1), (3, 2))
    )

    @pl.when(jnp.logical_not(cross_ok))
    def _():
        for p in range(4, 7):

            @pl.loop(0, R + 2)
            def _(r):
                cbuf[p, r] = jnp.zeros((8, X), F32)

    @pl.loop(0, max(CH + FAR, len(items)))
    def _(n):
        for ch in range(2):
            i = n - off[ch]

            @pl.when(jnp.logical_and(cross_ok, jnp.logical_and(i >= 0, i < CH)))
            def _():
                relay(ch, i).wait_recv()

                @pl.when(sends_on[ch])
                def _():
                    relay(ch, i).start()

        for group in range(0, len(items), 8):

            @pl.when(jnp.logical_and(n >= group, n < group + 8))
            def _():
                for m, work in enumerate(items[group : group + 8]):
                    if work is not None:
                        pl.when(n == group + m)(work)

    to_partner(0).wait_recv()
    to_partner(1).wait_recv()

    def o_send(e):
        sp = col * 4 + (e // 4) * 2 + zhi
        te = e % 4
        return (
            jnp.logical_and(sp == s, te == t),
            own.at[pl.ds(2 * e, 2)],
            go.at[t, core],
            gos.at[e],
            gor.at[t],
            dev(te, sp),
        )

    def x_send(e):
        sp = qcol * 4 + (e // 4) * 2 + qzhi
        te = e % 4
        return (
            jnp.logical_and(sp == s, te == t),
            ext.at[pl.ds(2 * e, 2)],
            gx.at[qcore, t],
            gxs.at[e],
            gxr.at[qcore, t],
            dev(te, sp),
        )

    def rows_and_sends(one_row, send):
        @pl.loop(0, 9)
        def _(i):
            @pl.when(i < 8)
            def _():
                e = (z + 4 + i) % 8
                one_row(2 * e)
                one_row(2 * e + 1)

            @pl.when(i > 0)
            def _():
                cross_send(*send((z + 3 + i) % 8))

    share_halos()
    rows_and_sends(own_row, o_send)
    after_plane(6)
    step_rest(2, 5, 5)

    @pl.when(cross_ok)
    def _():
        rows_and_sends(ext_row, x_send)

    c_halo(0).wait_recv()
    c_halo(1).wait_recv()

    @pl.when(next_ok)
    def _():
        c_halo(2).wait_recv()

    @pl.when(prev_ok)
    def _():
        c_halo(3).wait_recv()

    for j in range(2):

        @pl.when(jnp.logical_not(side_ok[j]))
        def _():
            cco[j] = jnp.zeros((2, 8, X), F32)
            gx[j] = jnp.zeros((4, 2, 8, X), F32)

    def arrived(g):
        pltpu.make_async_copy(go.at[g], go.at[g], gor.at[g]).wait()
        for j in range(2):

            @pl.when(side_ok[j])
            def _():
                pltpu.make_async_copy(gx.at[j, g], gx.at[j, g], gxr.at[j, g]).wait()

    def e_halo(k, kind):
        src, dst = (
            (eb.at[k, 0], hhi.at[k]),
            (eb.at[k, 1], hlo.at[k]),
            (eb.at[k, :, 0], hn.at[k]),
            (eb.at[k, :, 1], hp.at[k]),
        )[kind]
        return pltpu.make_async_remote_copy(
            src_ref=src,
            dst_ref=dst,
            send_sem=hs.at[k, kind],
            recv_sem=hr.at[k, kind],
            device_id=beside[kind],
            device_id_type=MESH,
        )

    def e_back(k, j):
        sp = col * 4 + core * 2 + j
        return (
            jnp.logical_and(sp == s, t == k),
            eb.at[k, :, j],
            eout.at[pl.ds(2 * z, 2)],
            eos.at[k, j],
            eor.at[0],
            dev(k, sp),
        )

    arrived(3)
    for b in range(2):
        for j in range(2):
            eb[0, b, j] = go[3, j, b] + gx[j, 3, b]

    def send_level(k):
        if k < 3:
            e_halo(k, 0).start()
            e_halo(k, 1).start()

            @pl.when(prev_ok)
            def _():
                e_halo(k, 2).start()

            @pl.when(next_ok)
            def _():
                e_halo(k, 3).start()

        for j in range(2):
            cross_send(*e_back(k, j))

    send_level(0)
    for k in range(3):
        arrived(k)
        e_halo(k, 0).wait_recv()
        e_halo(k, 1).wait_recv()

        @pl.when(next_ok)
        def _():
            e_halo(k, 2).wait_recv()

        @pl.when(prev_ok)
        def _():
            e_halo(k, 3).wait_recv()

        @pl.when(jnp.logical_not(next_ok))
        def _():
            hn[k] = jnp.zeros((2, 8, X), F32)

        @pl.when(jnp.logical_not(prev_ok))
        def _():
            hp[k] = jnp.zeros((2, 8, X), F32)

        for j in range(2):

            def wrapped(x, c, turn, at_end):
                return [jnp.where(at_end, turn(y), y) for y in row(x, *c)]

            vs = (
                wrapped(hlo, (k, j), from_above, z == 0),
                row(eb, k, 0, j),
                row(eb, k, 1, j),
                wrapped(hhi, (k, j), from_below, z == 7),
            )
            cs = (
                wrapped(ccb, (j, 0), from_above, z == 0),
                row(ccb, j, 1),
                row(ccb, j, 2),
                wrapped(ccb, (j, 3), from_below, z == 7),
            )
            for b in range(2):
                far = row(hp if j == 0 else hn, k, b)
                v_io = each(lambda x, y: jnp.where(even(), x, y), row(eb, k, b, 1 - j), far)
                c_io = each(lambda x, y: jnp.where(even(), x, y), row(ccb, 1 - j, b + 1), row(cco, j, b))
                new = coarse_advance(
                    cs[b + 1], cs[b + 2], cs[b], c_io, vs[b + 1], vs[b + 2], vs[b], v_io
                )
                put(eb, add(new, add(row(go, k, j, b), row(gx, j, k, b))), k + 1, b, j)
        send_level(k + 1)

    pltpu.make_async_copy(eout, eout, eor.at[0]).wait()

    @pl.loop(0, RC, unroll=4)
    def _(r):
        here = eout[r]
        wide[2 * r] = here
        wide[2 * r + 1] = here

    for sl in range(8):
        pltpu.make_async_copy(wide.at[:, sl, :], out.at[pl.ds(R * sl, R), :], ld_sem.at[0]).start()

    inner_c().wait_send()
    for k in range(STEPS - 2, STEPS):
        inner_state(k).wait_send()
    for i in range(2):
        to_partner(i).wait_send()

    @pl.when(cross_ok)
    def _():
        for ch in range(2):

            @pl.when(starts[ch])
            def _():
                @pl.loop(0, CH)
                def _(i):
                    first(ch, i).wait_send()

            @pl.when(sends_on[ch])
            def _():
                @pl.loop(0, CH)
                def _(i):
                    relay(ch, i).wait_send()

    for h in range(2):
        cross_sent(*cc_own(h))
    c_halo(0).wait_send()
    c_halo(1).wait_send()

    @pl.when(prev_ok)
    def _():
        c_halo(2).wait_send()

    @pl.when(next_ok)
    def _():
        c_halo(3).wait_send()

    @pl.loop(0, 8)
    def _(e):
        cross_sent(*o_send(e))

        @pl.when(cross_ok)
        def _():
            cross_sent(*x_send(e))

    for k in range(3):
        e_halo(k, 0).wait_send()
        e_halo(k, 1).wait_send()

        @pl.when(prev_ok)
        def _():
            e_halo(k, 2).wait_send()

        @pl.when(next_ok)
        def _():
            e_halo(k, 3).wait_send()

    for k in range(4):
        for j in range(2):
            cross_sent(*e_back(k, j))
    pltpu.make_async_copy(out, out, ld_sem.at[0]).wait()


def final_kernel(itr, e, out, res, osem):
    core = lax.axis_index("space") % 2

    def plane(p):
        return (3 - p) + core * (2 * p - 3)

    first = (subs((8, 128)) & 1) == 0

    def row_pairs(v):
        return [x + jnp.where(first, pltpu.roll(x, 7, axis=0), pltpu.roll(x, 1, axis=0)) for x in v]

    def store(n):
        return pltpu.make_async_copy(res.at[n], out.at[0, :, pl.ds(PART * n, PART), :], osem.at[n])

    for n in range(Y // PART):

        @pl.loop(0, PART // 8, unroll=2)
        def _(i):
            at = pl.ds(pl.multiple_of(PART * n + 8 * i, 8), 8)
            here = pl.ds(pl.multiple_of(8 * i, 8), 8)
            tile = lambda ref, *k: [ref[(*k, slice(128 * q, 128 * q + 128))] for q in range(LT)]
            v = [tile(itr, 0, plane(p), at) for p in range(4)]
            mean = pack(row_pairs(add(v[0], v[1])), row_pairs(add(v[2], v[3])))
            d = each(lambda x, y: x - 0.125 * y, tile(e, at), mean)
            halves = (
                [jnp.where(even(), x, pltpu.roll(x, 1, axis=1)) for x in d],
                [jnp.where(even(), pltpu.roll(x, 127, axis=1), x) for x in d],
            )
            for p in range(4):
                new = add(v[p], halves[p // 2])
                for q in range(LT):
                    res[n, plane(p), here, 128 * q : 128 * q + 128] = new[q]

        store(n).start()
    for n in range(Y // PART):
        store(n).wait()


def local(initial, iterate, diffusivity):
    vm = lambda *shape: pltpu.VMEM(shape, F32)
    dma = lambda *shape: pltpu.SemaphoreType.DMA(shape)
    hbm = pl.BlockSpec(memory_space=pl.ANY)
    err = pl.pallas_call(
        main_kernel,
        out_shape=jax.ShapeDtypeStruct((Y, X), F32),
        in_specs=[hbm] * 3,
        out_specs=hbm,
        scratch_shapes=[
            vm(8, R + 2, 8, X),
            vm(7, R, 8, X),
            vm(7, R + 1, 8, X),
            vm(7, R, 8, X),
            vm(7, R, 8, 128),
            vm(7, R + 2, 8, X),
            vm(7, R + 2, 8, X),
            vm(STEPS, R, 8, X),
            vm(RC, 8, X),
            vm(RC, 8, X),
            vm(RC, 8, X),
            vm(RC, 8, X),
            vm(RC, 8, X),
            vm(RC, 8, X),
            vm(2, 4, 8, X),
            vm(2, 2, 8, X),
            vm(4, 2, 2, 8, X),
            vm(2, 4, 2, 8, X),
            vm(4, 2, 2, 8, X),
            vm(3, 2, 8, X),
            vm(3, 2, 8, X),
            vm(3, 2, 8, X),
            vm(3, 2, 8, X),
            vm(RC, 8, X),
            vm(R, 8, X),
            dma(2),
            dma(2),
            dma(4, CH),
            dma(2, CH),
            dma(STEPS),
            dma(STEPS),
            dma(2),
            dma(2),
            dma(2),
            dma(1),
            dma(4),
            dma(4),
            dma(8),
            dma(4),
            dma(8),
            dma(2, 4),
            dma(3, 4),
            dma(3, 4),
            dma(4, 2),
            dma(1),
        ],
        compiler_params=pltpu.CompilerParams(
            collective_id=0, has_side_effects=True, vmem_limit_bytes=60 * 2**20
        ),
    )(initial, iterate, diffusivity)
    return pl.pallas_call(
        final_kernel,
        out_shape=jax.ShapeDtypeStruct(iterate.shape, F32),
        in_specs=[pl.BlockSpec(memory_space=pltpu.VMEM)] * 2,
        out_specs=hbm,
        scratch_shapes=[vm(Y // PART, 4, PART, X), dma(Y // PART)],
        compiler_params=pltpu.CompilerParams(vmem_limit_bytes=16 * 2**20),
    )(iterate, err)


def solution(mesh):
    placed = (P("space", None, None), P("tm", "space", None, None), P("space", None, None))
    return jax.shard_map(
        local, mesh=mesh, in_specs=placed, out_specs=P("tm", "space", None, None), check_vma=False
    )
```

```python
import functools

import jax
import jax.numpy as jnp
from jax import lax
from jax.experimental import pallas as pl
from jax.experimental.pallas import tpu as pltpu
from jax.sharding import PartitionSpec as P

STEPS = 4
courant = 0.15
K = 0.5 * courant
F32 = jnp.float32
MESH = pl.DeviceIdType.MESH

Y, X = 256, 512
LT = X // 128
R = 32
RC = 16
CH = 24
LEAD, FAR = 5, 14
PART = 32


PER = CH // 3


def lane():
    return lax.broadcasted_iota(jnp.int32, (8, 128), 1)


def even():
    return (lane() & 1) == 0


def subs(shape):
    return lax.broadcasted_iota(jnp.int32, shape, 0)


def from_below(v):
    return jnp.where(subs(v.shape) == 7, 0.0, pltpu.roll(v, 7, axis=0))


def from_above(v):
    return jnp.where(subs(v.shape) == 0, 0.0, pltpu.roll(v, 1, axis=0))


def row(ref, *at):
    return [ref[(*at, slice(None), slice(128 * q, 128 * q + 128))] for q in range(LT)]


def put(ref, value, *at):
    for q in range(LT):
        ref[(*at, slice(None), slice(128 * q, 128 * q + 128))] = value[q]


def each(f, *rows):
    return [f(*t) for t in zip(*rows)]


def add(a, b):
    return each(lambda x, y: x + y, a, b)


def sub(a, b):
    return each(lambda x, y: x - y, a, b)


def mul(a, b):
    return each(lambda x, y: x * y, a, b)


def at_right(v, by=1):
    turned = [pltpu.roll(x, 128 - by, axis=1) for x in v] + [jnp.zeros((8, 128), F32)]
    return [jnp.where(lane() >= 128 - by, turned[q + 1], turned[q]) for q in range(LT)]


def at_left(v, by=1, first=None):
    turned = [jnp.zeros((8, 128), F32) if first is None else first] + [pltpu.roll(x, by, axis=1) for x in v]
    return [jnp.where(lane() < by, turned[q], turned[q + 1]) for q in range(LT)]


def swap_pairs(v):
    return [jnp.where(even(), pltpu.roll(x, 127, axis=1), pltpu.roll(x, 1, axis=1)) for x in v]


def pack(a, b):
    return each(
        lambda x, y: jnp.where(even(), x + pltpu.roll(x, 127, axis=1), y + pltpu.roll(y, 1, axis=1)), a, b
    )


def coarse_advance(c, c_up, c_dn, c_io, v, v_up, v_dn, v_io):
    flux = None
    for cn, vn in (
        (at_right(c, 2), at_right(v, 2)),
        (at_left(c, 2), at_left(v, 2)),
        (c_up, v_up),
        (c_dn, v_dn),
        (swap_pairs(c), swap_pairs(v)),
        (c_io, v_io),
    ):
        term = mul(add(c, cn), sub(vn, v))
        flux = term if flux is None else add(flux, term)
    return each(lambda x, f: x + K * f, v, flux)


def main_kernel(
    ini,
    itr,
    dif,
    out,
    cbuf,
    kx,
    ky,
    kz,
    kl,
    wa,
    wb,
    inn,
    cc,
    ccp,
    icoarse,
    ipart,
    own,
    ext,
    ccb,
    cco,
    go,
    gx,
    eb,
    hlo,
    hhi,
    hp,
    hn,
    eout,
    wide,
    ld_sem,
    icp,
    chs,
    chr_,
    ins,
    inr,
    pps,
    ppr,
    cbs,
    cbr,
    cos,
    cor,
    gos,
    gor,
    gxs,
    gxr,
    hs,
    hr,
    eos,
    eor,
):
    t = lax.axis_index("tm")
    s = lax.axis_index("space")
    core = s % 2
    zhi = (s // 2) % 2
    col = s // 4
    z = zhi * 4 + t
    ncol = lax.axis_size("space") // 4
    partner = s + 1 - 2 * core
    cross_ok = jnp.logical_and(
        jnp.logical_or(core == 1, s > 0), jnp.logical_or(core == 0, s < 4 * ncol - 1)
    )
    cross = jnp.where(cross_ok, s - 1 + 2 * core, s)
    qcol = cross // 4
    qzhi = (cross // 2) % 2
    qcore = cross % 2

    states = (wa, wb)

    def plane(p):
        return (3 - p) + core * (2 * p - 3)

    def dev(tt, ss):
        return {"tm": tt, "space": ss}

    barrier = pltpu.get_barrier_semaphore()

    @pl.loop(0, 16)
    def _(i):
        ti, si = i % 4, col * 4 + i // 4

        @pl.when(jnp.logical_not(jnp.logical_and(ti == t, si == s)))
        def _():
            pl.semaphore_signal(barrier, inc=1, device_id=dev(ti, si), device_id_type=MESH)

    lat_ok = jnp.logical_or(
        jnp.logical_and(core == 0, col > 0), jnp.logical_and(core == 1, col < ncol - 1)
    )
    lat_col = jnp.where(core == 0, col - 1, col + 1)

    @pl.when(lat_ok)
    def _():
        @pl.loop(0, 8)
        def _(i):
            si = lat_col * 4 + (i // 4) * 2 + 1 - core
            pl.semaphore_signal(barrier, inc=1, device_id=dev(i % 4, si), device_id_type=MESH)

    def load_rows(src, dst, sem):
        @pl.loop(0, 4)
        def _(p):
            for sl in range(8):
                pltpu.make_async_copy(
                    src.at[plane(p), pl.ds(R * sl, R), :], dst.at[p, pl.ds(1, R), sl, :], sem
                ).start()

    load_rows(dif, cbuf, ld_sem.at[0])

    @pl.when(t == 3)
    def _():
        load_rows(ini, wa, ld_sem.at[1])

    @pl.when(t != 3)
    def _():
        load_rows(itr.at[0], wa, ld_sem.at[1])

    held_c = cbuf.at[pl.ds(0, 4), pl.ds(1, R)]
    pltpu.make_async_copy(held_c, held_c, ld_sem.at[0]).wait()

    pl.semaphore_wait(barrier, jnp.where(lat_ok, 23, 15))

    def inner_c():
        return pltpu.make_async_remote_copy(
            src_ref=cbuf.at[0, pl.ds(1, R)],
            dst_ref=cbuf.at[7, pl.ds(1, R)],
            send_sem=icp.at[0],
            recv_sem=icp.at[1],
            device_id=dev(t, partner),
            device_id_type=MESH,
        )

    inner_c().start()

    def piece(j, ch, i):
        return cbuf.at[j, pl.ds(1 + (R // 2) * ch + (i % PER) * (R // 2 // PER), R // 2 // PER)]

    def first(ch, i):
        j = i // PER
        return pltpu.make_async_remote_copy(
            src_ref=piece(3 - j, ch, i),
            dst_ref=piece(4 + j, ch, i),
            send_sem=chs.at[2 + ch, i],
            recv_sem=chr_.at[ch, i],
            device_id=dev(3 - 3 * ch, cross),
            device_id_type=MESH,
        )

    def relay(ch, i):
        ref = piece(4 + i // PER, ch, i)
        return pltpu.make_async_remote_copy(
            src_ref=ref,
            dst_ref=ref,
            send_sem=chs.at[ch, i],
            recv_sem=chr_.at[ch, i],
            device_id=dev(jnp.clip(t - 1 + 2 * ch, 0, 3), s),
            device_id_type=MESH,
        )

    starts = (t == 0, t == 3)
    sends_on = (t > 0, t < 3)

    @pl.when(cross_ok)
    def _():
        for ch in range(2):

            @pl.when(starts[ch])
            def _():
                @pl.loop(0, CH)
                def _(i):
                    first(ch, i).start()

    def edge_rows(dst, d):
        dst[d, 0] = from_above(dst[d, R])
        dst[d, R + 1] = from_below(dst[d, 1])

    held_u = wa.at[pl.ds(0, 4), pl.ds(1, R)]
    pltpu.make_async_copy(held_u, held_u, ld_sem.at[1]).wait()

    def inner_state(k):
        return pltpu.make_async_remote_copy(
            src_ref=states[k % 2].at[0, pl.ds(1, R)],
            dst_ref=inn.at[k],
            send_sem=ins.at[k],
            recv_sem=inr.at[k],
            device_id=dev(t, partner),
            device_id_type=MESH,
        )

    inner_state(0).start()
    for p in range(4):
        edge_rows(wa, p)
        edge_rows(cbuf, p)

    def to_partner(i):
        src, dst = ((cc, ccp), (icoarse, ipart))[i]
        return pltpu.make_async_remote_copy(
            src_ref=src,
            dst_ref=dst,
            send_sem=pps.at[i],
            recv_sem=ppr.at[i],
            device_id=dev(t, partner),
            device_id_type=MESH,
        )

    def cross_send(is_self, src, dst, ssem, rsem, to):
        @pl.when(is_self)
        def _():
            pltpu.make_async_copy(src, dst, rsem).start()

        @pl.when(jnp.logical_not(is_self))
        def _():
            pltpu.make_async_remote_copy(
                src_ref=src,
                dst_ref=dst,
                send_sem=ssem,
                recv_sem=rsem,
                device_id=to,
                device_id_type=MESH,
            ).start()

    def cross_sent(is_self, src, dst, ssem, rsem, to):
        @pl.when(jnp.logical_not(is_self))
        def _():
            pltpu.make_async_remote_copy(
                src_ref=src,
                dst_ref=dst,
                send_sem=ssem,
                recv_sem=rsem,
                device_id=to,
                device_id_type=MESH,
            ).wait_send()

    def cc_own(h):
        e = t + 4 * h
        sp = col * 4 + h * 2 + zhi
        return (
            sp == s,
            cc.at[pl.ds(2 * e, 2)],
            ccb.at[core, pl.ds(1, 2)],
            cbs.at[h],
            cbr.at[0],
            dev(t, sp),
        )

    prev_ok = jnp.logical_or(core == 1, col > 0)
    next_ok = jnp.logical_or(core == 0, col < ncol - 1)
    prev_sp = jnp.where(core == 1, s - 1, jnp.maximum(col - 1, 0) * 4 + zhi * 2 + 1)
    next_sp = jnp.where(core == 0, s + 1, jnp.minimum(col + 1, ncol - 1) * 4 + zhi * 2)
    side_ok = (prev_ok, next_ok)

    zu, zd = (z + 1) % 8, (z + 7) % 8
    beside = (
        dev(zd % 4, col * 4 + (zd // 4) * 2 + core),
        dev(zu % 4, col * 4 + (zu // 4) * 2 + core),
        dev(t, prev_sp),
        dev(t, next_sp),
    )

    def c_halo(kind):
        src, dst = (
            (ccb.at[:, 1], ccb.at[:, 3]),
            (ccb.at[:, 2], ccb.at[:, 0]),
            (ccb.at[0, pl.ds(1, 2)], cco.at[1]),
            (ccb.at[1, pl.ds(1, 2)], cco.at[0]),
        )[kind]
        return pltpu.make_async_remote_copy(
            src_ref=src,
            dst_ref=dst,
            send_sem=cos.at[kind],
            recv_sem=cor.at[kind],
            device_id=beside[kind],
            device_id_type=MESH,
        )

    def share_halos():
        held = ccb.at[:, pl.ds(1, 2)]
        pltpu.make_async_copy(held, held, cbr.at[0]).wait()
        c_halo(0).start()
        c_halo(1).start()

        @pl.when(prev_ok)
        def _():
            c_halo(2).start()

        @pl.when(next_ok)
        def _():
            c_halo(3).start()

    vflag = jnp.where(cross_ok, 1.0, 0.0).astype(F32)
    gflag = jnp.where(t == 3, 0.0, 1.0).astype(F32)

    def coefficients(p):
        @pl.loop(0, R, unroll=4)
        def _(r):
            c = row(cbuf, p, r + 1)
            face = lambda n: each(lambda x, y: K * (x + y), c, n)
            put(kx, face(at_right(c)), p, r)
            put(ky, face(row(cbuf, p, r)), p, r)
            put(kz, face(row(cbuf, (p + 7) % 8, r + 1)), p, r)
            kl[p, r] = K * c[0]

        ky[p, R] = K * (cbuf[p, R] + cbuf[p, R + 1])

    def flux(coeff, a, b):
        return mul(coeff, sub(a, b))

    def step_inner(k, lo=0, hi=R // 2):
        src, dst = states[k % 2], states[(k + 1) % 2]
        if lo == 0:
            inner_state(k).wait_recv()
            if k > 0:
                inner_state(k - 1).wait_send()
        step_planes(k, src, dst, 0, 0, lo, hi)
        if hi == R // 2:
            edge_rows(dst, 0)
            inner_state(k + 1).start()

    def step_rest(k, first, last, lo=0, hi=R // 2):
        src, dst = states[k % 2], states[(k + 1) % 2]
        step_planes(k, src, dst, first, last, lo, hi)
        if hi < R // 2:
            return
        for p in range(first, last + 1 + (last == 3 + k)):
            edge_rows(dst, p)

    def step_planes(k, src, dst, first, last, lo, hi):
        top = 3 + k

        @pl.loop(lo, hi, unroll=4)
        def _(i):
            r = 2 * i
            below = [row(inn, k, r + j) if first == 0 else row(src, first - 1, r + j + 1) for j in range(2)]
            v = [row(src, first, r + j + 1) for j in range(2)]
            fz = [flux(row(kz, first, r + j), v[j], below[j]) for j in range(2)]
            for p in range(first, last + 1):
                above = None
                if p < top:
                    above = [row(src, p + 1, r + j + 1) for j in range(2)]
                around = [row(src, p, r)] + v + [row(src, p, r + 3)]
                fy = [flux(row(ky, p, r + j), around[j + 1], around[j]) for j in range(3)]
                fz_next = []
                for j in range(2):
                    fx = flux(row(kx, p, r + j), at_right(v[j]), v[j])
                    total = sub(fx, at_left(fx, 1, kl[p, r + j] * v[j][0]))
                    total = add(total, sub(fy[j + 1], fy[j]))
                    if above is None:
                        out_flow = mul(row(kz, p + 1, r + j), v[j])
                        total = sub(total, add(out_flow, fz[j]))
                        if top == 3:
                            out_flow = [vflag * x for x in out_flow]
                        put(dst, out_flow, p + 1, r + j + 1)
                    else:
                        fz_next.append(flux(row(kz, p + 1, r + j), above[j], v[j]))
                        total = add(total, sub(fz_next[j], fz[j]))
                    new = add(v[j], total)
                    if p == 4:
                        new = [vflag * x for x in new]
                    put(dst, new, p, r + j + 1)
                v, fz = above, fz_next

    def restricted():
        @pl.loop(0, RC, unroll=2)
        def _(r):
            def block(src, p):
                a = 2 * r + 1
                return add(add(row(src, p, a), row(src, p, a + 1)), add(row(src, p + 1, a), row(src, p + 1, a + 1)))

            put(cc, [0.125 * x for x in pack(block(cbuf, 0), block(cbuf, 2))], r)
            put(icoarse, [0.125 * x for x in pack(block(wa, 0), block(wa, 2))], r)

    def own_first():
        inner_c().wait_recv()
        edge_rows(cbuf, 7)
        coefficients(0)

    def share_coarse():
        to_partner(0).start()
        to_partner(1).start()
        for h in range(2):
            cross_send(*cc_own(h))

    def after_plane(p):
        edge_rows(cbuf, p)
        coefficients(p)

    def last_groups(r, groups, low):
        src = states[(STEPS - 1) % 2]
        ends = []
        v = [row(src, groups[0][0], r + j + 1) for j in range(2)]
        low = [flux(row(kz, groups[0][0], r + j), v[j], low(j)) for j in range(2)]
        low = add(low[0], low[1])
        for planes in groups:
            held = fxs = net = kls = None
            for p in planes:
                fy = sub(
                    flux(row(ky, p, r + 2), row(src, p, r + 3), v[1]), flux(row(ky, p, r), v[0], row(src, p, r))
                )
                net = fy if net is None else add(net, fy)
                for j in range(2):
                    fx = flux(row(kx, p, r + j), at_right(v[j]), v[j])
                    fl = kl[p, r + j] * v[j][0]
                    fxs = fx if fxs is None else add(fxs, fx)
                    kls = fl if kls is None else kls + fl
                both = add(v[0], v[1])
                held = both if held is None else add(held, both)
                if p < 6:
                    last_v, v = v, [row(src, p + 1, r + j + 1) for j in range(2)]
            net = sub(net, low)
            if planes[-1] < 6:
                high = [flux(row(kz, planes[-1] + 1, r + j), v[j], last_v[j]) for j in range(2)]
                low = add(high[0], high[1])
                net = add(net, low)
            held = add(held, net)
            right = [pltpu.roll(x, 127, axis=1) for x in add(held, fxs)]
            ends.append(sub(add(held, right), at_left(fxs, 1, kls)))
        return ends

    def packed(a, b):
        return each(lambda x, y: 0.125 * jnp.where(even(), x, pltpu.roll(y, 1, axis=1)), a, b)

    def coarse_side(rc):
        a = 2 * rc + 1
        outer = add(add(row(cbuf, 4, a), row(cbuf, 4, a + 1)), add(row(cbuf, 5, a), row(cbuf, 5, a + 1)))
        return each(lambda x, y: jnp.where(even(), x, 0.125 * y), row(ccp, rc), pack(outer, outer))

    def inner_rows(lo, hi):
        if lo == 0:
            inner_state(STEPS - 1).wait_recv()

        @pl.loop(lo, hi, unroll=2)
        def _(rc):
            put(own, last_groups(2 * rc, ((0, 1),), lambda j: row(inn, STEPS - 1, 2 * rc + j))[0], rc)

    def own_row(rc):
        lo = jnp.maximum(rc - 1, 0)
        hi = jnp.minimum(rc + 1, RC - 1)

        def neighbours(ref):
            up = each(lambda x, y: jnp.where(rc == RC - 1, from_below(y), x), row(ref, hi), row(ref, 0))
            dn = each(lambda x, y: jnp.where(rc == 0, from_above(y), x), row(ref, lo), row(ref, RC - 1))
            return up, dn

        src = states[(STEPS - 1) % 2]
        ends = last_groups(2 * rc, ((2, 3),), lambda j: row(src, 1, 2 * rc + j + 1))
        c_up, c_dn = neighbours(cc)
        u_up, u_dn = neighbours(icoarse)
        u_io = [jnp.where(even(), x, 0.0) for x in row(ipart, rc)]
        back = coarse_advance(
            row(cc, rc), c_up, c_dn, coarse_side(rc), row(icoarse, rc), u_up, u_dn, u_io
        )
        put(own, each(lambda x, y: x - gflag * y, packed(row(own, rc), ends[0]), back), rc)

    def ext_row(rc):
        src = states[(STEPS - 1) % 2]
        ends = last_groups(2 * rc, ((4, 5), (6,)), lambda j: row(src, 3, 2 * rc + j + 1))
        lost = each(
            lambda x, y, z: jnp.where(even(), 0.0, K * (x + y) * z),
            row(cc, rc),
            coarse_side(rc),
            row(icoarse, rc),
        )
        put(ext, each(lambda x, y: x - gflag * y, packed(ends[1], ends[0]), lost), rc)

    def parts(f, *args, n):
        cuts = [R // 2 * i // n for i in range(n + 1)]
        return [functools.partial(f, *args, lo, hi) for lo, hi in zip(cuts, cuts[1:])]

    first_items = [functools.partial(coefficients, p) for p in (1, 2, 3)] + parts(step_inner, 0, n=2)
    items = [
        *parts(step_rest, 0, 1, 2, n=4),
        *parts(step_inner, 1, n=2),
        *parts(step_rest, 1, 1, 1, n=2),
        *parts(step_inner, 2, n=2),
    ]
    items += [None] * (PER - 1 + FAR - len(first_items) - len(items))
    items += [
        functools.partial(after_plane, 4),
        *parts(step_rest, 0, 3, 3, n=2),
        *parts(step_rest, 1, 2, 3, n=4),
        *parts(step_rest, 2, 1, 2, n=4),
        *parts(inner_rows, n=4),
        functools.partial(after_plane, 5),
        *parts(step_rest, 1, 4, 4, n=2),
        *parts(step_rest, 2, 3, 4, n=4),
    ]
    middle = jnp.logical_or(t == 1, t == 2)
    restricted()
    share_coarse()
    own_first()

    @pl.when(middle)
    def _():
        for work in first_items:
            work()

    def on_ends(work):
        return lambda: pl.when(jnp.logical_not(middle))(work)

    items = [on_ends(work) for work in first_items] + items

    off = tuple(
        jnp.where(t == last, FAR, jnp.where(t == near, LEAD, 0)) for last, near in ((0, 1), (3, 2))
    )

    @pl.when(jnp.logical_not(cross_ok))
    def _():
        for p in range(4, 7):

            @pl.loop(0, R + 2)
            def _(r):
                cbuf[p, r] = jnp.zeros((8, X), F32)

    @pl.loop(0, max(CH + FAR, len(items)))
    def _(n):
        for ch in range(2):
            i = n - off[ch]

            @pl.when(jnp.logical_and(cross_ok, jnp.logical_and(i >= 0, i < CH)))
            def _():
                relay(ch, i).wait_recv()

                @pl.when(sends_on[ch])
                def _():
                    relay(ch, i).start()

        for group in range(0, len(items), 8):

            @pl.when(jnp.logical_and(n >= group, n < group + 8))
            def _():
                for m, work in enumerate(items[group : group + 8]):
                    if work is not None:
                        pl.when(n == group + m)(work)

    to_partner(0).wait_recv()
    to_partner(1).wait_recv()

    def o_send(e):
        sp = col * 4 + (e // 4) * 2 + zhi
        te = e % 4
        return (
            jnp.logical_and(sp == s, te == t),
            own.at[pl.ds(2 * e, 2)],
            go.at[t, core],
            gos.at[e],
            gor.at[t],
            dev(te, sp),
        )

    def x_send(e):
        sp = qcol * 4 + (e // 4) * 2 + qzhi
        te = e % 4
        return (
            jnp.logical_and(sp == s, te == t),
            ext.at[pl.ds(2 * e, 2)],
            gx.at[qcore, t],
            gxs.at[e],
            gxr.at[qcore, t],
            dev(te, sp),
        )

    def rows_and_sends(one_row, send):
        @pl.loop(0, 9)
        def _(i):
            @pl.when(i < 8)
            def _():
                e = (z + 4 + i) % 8
                one_row(2 * e)
                one_row(2 * e + 1)

            @pl.when(i > 0)
            def _():
                cross_send(*send((z + 3 + i) % 8))

    share_halos()
    rows_and_sends(own_row, o_send)
    after_plane(6)
    step_rest(2, 5, 5)

    @pl.when(cross_ok)
    def _():
        rows_and_sends(ext_row, x_send)

    c_halo(0).wait_recv()
    c_halo(1).wait_recv()

    @pl.when(next_ok)
    def _():
        c_halo(2).wait_recv()

    @pl.when(prev_ok)
    def _():
        c_halo(3).wait_recv()

    for j in range(2):

        @pl.when(jnp.logical_not(side_ok[j]))
        def _():
            cco[j] = jnp.zeros((2, 8, X), F32)
            gx[j] = jnp.zeros((4, 2, 8, X), F32)

    def arrived(g):
        pltpu.make_async_copy(go.at[g], go.at[g], gor.at[g]).wait()
        for j in range(2):

            @pl.when(side_ok[j])
            def _():
                pltpu.make_async_copy(gx.at[j, g], gx.at[j, g], gxr.at[j, g]).wait()

    def e_halo(k, kind):
        src, dst = (
            (eb.at[k, 0], hhi.at[k]),
            (eb.at[k, 1], hlo.at[k]),
            (eb.at[k, :, 0], hn.at[k]),
            (eb.at[k, :, 1], hp.at[k]),
        )[kind]
        return pltpu.make_async_remote_copy(
            src_ref=src,
            dst_ref=dst,
            send_sem=hs.at[k, kind],
            recv_sem=hr.at[k, kind],
            device_id=beside[kind],
            device_id_type=MESH,
        )

    def e_back(k, j):
        sp = col * 4 + core * 2 + j
        return (
            jnp.logical_and(sp == s, t == k),
            eb.at[k, :, j],
            eout.at[pl.ds(2 * z, 2)],
            eos.at[k, j],
            eor.at[0],
            dev(k, sp),
        )

    arrived(3)
    for b in range(2):
        for j in range(2):
            eb[0, b, j] = go[3, j, b] + gx[j, 3, b]

    def send_level(k):
        if k < 3:
            e_halo(k, 0).start()
            e_halo(k, 1).start()

            @pl.when(prev_ok)
            def _():
                e_halo(k, 2).start()

            @pl.when(next_ok)
            def _():
                e_halo(k, 3).start()

        for j in range(2):
            cross_send(*e_back(k, j))

    send_level(0)
    for k in range(3):
        arrived(k)
        e_halo(k, 0).wait_recv()
        e_halo(k, 1).wait_recv()

        @pl.when(next_ok)
        def _():
            e_halo(k, 2).wait_recv()

        @pl.when(prev_ok)
        def _():
            e_halo(k, 3).wait_recv()

        @pl.when(jnp.logical_not(next_ok))
        def _():
            hn[k] = jnp.zeros((2, 8, X), F32)

        @pl.when(jnp.logical_not(prev_ok))
        def _():
            hp[k] = jnp.zeros((2, 8, X), F32)

        for j in range(2):

            def wrapped(x, c, turn, at_end):
                return [jnp.where(at_end, turn(y), y) for y in row(x, *c)]

            vs = (
                wrapped(hlo, (k, j), from_above, z == 0),
                row(eb, k, 0, j),
                row(eb, k, 1, j),
                wrapped(hhi, (k, j), from_below, z == 7),
            )
            cs = (
                wrapped(ccb, (j, 0), from_above, z == 0),
                row(ccb, j, 1),
                row(ccb, j, 2),
                wrapped(ccb, (j, 3), from_below, z == 7),
            )
            for b in range(2):
                far = row(hp if j == 0 else hn, k, b)
                v_io = each(lambda x, y: jnp.where(even(), x, y), row(eb, k, b, 1 - j), far)
                c_io = each(lambda x, y: jnp.where(even(), x, y), row(ccb, 1 - j, b + 1), row(cco, j, b))
                new = coarse_advance(
                    cs[b + 1], cs[b + 2], cs[b], c_io, vs[b + 1], vs[b + 2], vs[b], v_io
                )
                put(eb, add(new, add(row(go, k, j, b), row(gx, j, k, b))), k + 1, b, j)
        send_level(k + 1)

    pltpu.make_async_copy(eout, eout, eor.at[0]).wait()

    @pl.loop(0, RC, unroll=4)
    def _(r):
        here = eout[r]
        wide[2 * r] = here
        wide[2 * r + 1] = here

    for sl in range(8):
        pltpu.make_async_copy(wide.at[:, sl, :], out.at[pl.ds(R * sl, R), :], ld_sem.at[0]).start()

    inner_c().wait_send()
    for k in range(STEPS - 2, STEPS):
        inner_state(k).wait_send()
    for i in range(2):
        to_partner(i).wait_send()

    @pl.when(cross_ok)
    def _():
        for ch in range(2):

            @pl.when(starts[ch])
            def _():
                @pl.loop(0, CH)
                def _(i):
                    first(ch, i).wait_send()

            @pl.when(sends_on[ch])
            def _():
                @pl.loop(0, CH)
                def _(i):
                    relay(ch, i).wait_send()

    for h in range(2):
        cross_sent(*cc_own(h))
    c_halo(0).wait_send()
    c_halo(1).wait_send()

    @pl.when(prev_ok)
    def _():
        c_halo(2).wait_send()

    @pl.when(next_ok)
    def _():
        c_halo(3).wait_send()

    @pl.loop(0, 8)
    def _(e):
        cross_sent(*o_send(e))

        @pl.when(cross_ok)
        def _():
            cross_sent(*x_send(e))

    for k in range(3):
        e_halo(k, 0).wait_send()
        e_halo(k, 1).wait_send()

        @pl.when(prev_ok)
        def _():
            e_halo(k, 2).wait_send()

        @pl.when(next_ok)
        def _():
            e_halo(k, 3).wait_send()

    for k in range(4):
        for j in range(2):
            cross_sent(*e_back(k, j))
    pltpu.make_async_copy(out, out, ld_sem.at[0]).wait()


def final_kernel(itr, e, out, res, osem):
    core = lax.axis_index("space") % 2

    def plane(p):
        return (3 - p) + core * (2 * p - 3)

    first = (subs((8, 128)) & 1) == 0

    def row_pairs(v):
        return [x + jnp.where(first, pltpu.roll(x, 7, axis=0), pltpu.roll(x, 1, axis=0)) for x in v]

    def store(n):
        return pltpu.make_async_copy(res.at[n], out.at[0, :, pl.ds(PART * n, PART), :], osem.at[n])

    for n in range(Y // PART):

        @pl.loop(0, PART // 8, unroll=4)
        def _(i):
            at = pl.ds(pl.multiple_of(PART * n + 8 * i, 8), 8)
            here = pl.ds(pl.multiple_of(8 * i, 8), 8)
            tile = lambda ref, *k: [ref[(*k, slice(128 * q, 128 * q + 128))] for q in range(LT)]
            v = [tile(itr, 0, plane(p), at) for p in range(4)]
            mean = pack(row_pairs(add(v[0], v[1])), row_pairs(add(v[2], v[3])))
            d = each(lambda x, y: x - 0.125 * y, tile(e, at), mean)
            halves = (
                [jnp.where(even(), x, pltpu.roll(x, 1, axis=1)) for x in d],
                [jnp.where(even(), pltpu.roll(x, 127, axis=1), x) for x in d],
            )
            for p in range(4):
                new = add(v[p], halves[p // 2])
                for q in range(LT):
                    res[n, plane(p), here, 128 * q : 128 * q + 128] = new[q]

        store(n).start()
    for n in range(Y // PART):
        store(n).wait()


def local(initial, iterate, diffusivity):
    vm = lambda *shape: pltpu.VMEM(shape, F32)
    dma = lambda *shape: pltpu.SemaphoreType.DMA(shape)
    hbm = pl.BlockSpec(memory_space=pl.ANY)
    err = pl.pallas_call(
        main_kernel,
        out_shape=jax.ShapeDtypeStruct((Y, X), F32),
        in_specs=[hbm] * 3,
        out_specs=hbm,
        scratch_shapes=[
            vm(8, R + 2, 8, X),
            vm(7, R, 8, X),
            vm(7, R + 1, 8, X),
            vm(7, R, 8, X),
            vm(7, R, 8, 128),
            vm(7, R + 2, 8, X),
            vm(7, R + 2, 8, X),
            vm(STEPS, R, 8, X),
            vm(RC, 8, X),
            vm(RC, 8, X),
            vm(RC, 8, X),
            vm(RC, 8, X),
            vm(RC, 8, X),
            vm(RC, 8, X),
            vm(2, 4, 8, X),
            vm(2, 2, 8, X),
            vm(4, 2, 2, 8, X),
            vm(2, 4, 2, 8, X),
            vm(4, 2, 2, 8, X),
            vm(3, 2, 8, X),
            vm(3, 2, 8, X),
            vm(3, 2, 8, X),
            vm(3, 2, 8, X),
            vm(RC, 8, X),
            vm(R, 8, X),
            dma(2),
            dma(2),
            dma(4, CH),
            dma(2, CH),
            dma(STEPS),
            dma(STEPS),
            dma(2),
            dma(2),
            dma(2),
            dma(1),
            dma(4),
            dma(4),
            dma(8),
            dma(4),
            dma(8),
            dma(2, 4),
            dma(3, 4),
            dma(3, 4),
            dma(4, 2),
            dma(1),
        ],
        compiler_params=pltpu.CompilerParams(
            collective_id=0, has_side_effects=True, vmem_limit_bytes=60 * 2**20
        ),
    )(initial, iterate, diffusivity)
    return pl.pallas_call(
        final_kernel,
        out_shape=jax.ShapeDtypeStruct(iterate.shape, F32),
        in_specs=[pl.BlockSpec(memory_space=pltpu.VMEM)] * 2,
        out_specs=hbm,
        scratch_shapes=[vm(Y // PART, 4, PART, X), dma(Y // PART)],
        compiler_params=pltpu.CompilerParams(vmem_limit_bytes=16 * 2**20),
    )(iterate, err)


def solution(mesh):
    placed = (P("space", None, None), P("tm", "space", None, None), P("space", None, None))
    return jax.shard_map(
        local, mesh=mesh, in_specs=placed, out_specs=P("tm", "space", None, None), check_vma=False
    )
```
